32 devices in a mesh: groups: 2 (over x), context: 16 (over z, y, core).
Axes of the slice: x: 2, y: 2, z: 4, core: 2. Of those that a mesh axis runs over, the one named last changes fastest.
Arguments:
- query_rows: bfloat16 [8192, 1536], P(('groups', 'context')), parts along dimension 0, may hold values from -9 to 9
- key_rows: bfloat16 [8192, 1536], P(('groups', 'context')), parts along dimension 0, may hold values from -9 to 9
- value_rows: bfloat16 [8192, 1536], P(('groups', 'context')), parts along dimension 0, may hold values from -6 to 6
- extents: int32 [12, 3], replicated, may hold values from 1 to 3, as said below
Outputs:
- attended: bfloat16 [8192, 1536], P(('groups', 'context')), parts along dimension 0
The draws below stay inside these ranges and needn't reach their ends.
There are 2 independent parts, one for each index of `groups`. The reference program is written for one: setup_inputs(seed, part) draws one part's arguments, and reference() takes and returns one part's arrays. A program takes and returns all parts, laid end to end along the dimension named above; an argument that names none is the same for every part. Nothing has to cross between parts.
Inputs may be any that keep to these rules, and one draw needn't show every extreme that they name: Every entry is 1 or 3; some head has extents 3, 3, 3.
All inputs are finite; a program needn't handle non-finite values.
Results may differ from the reference program's by a relative error of at most 0.004.
Values may be sent and summed in bfloat16 or wider, within the bound.
No kernel may reach another device: no remote copies, remote signals or barrier semaphores. Data moves between devices by JAX's collectives and lax.ppermute only.
A program may use at most 64 MiB of HBM per device.

```python
import math
import jax
import jax.numpy as jnp
from jax import lax

HEADS = 12
HD = 128
HT = 8
TILE_TOK = 256
SLAB_TOK = 256
TOKENS = 4096
CH = 1536
N_CONTEXT = 16


def shared_draw(key):
    query_key = jax.random.fold_in(key, 101)
    keys_key = jax.random.fold_in(key, 102)
    shape_full = (TOKENS, HEADS * HD)
    keys_out = jnp.clip(jax.random.normal(keys_key, shape_full, jnp.float32), -6.0, 6.0)
    query_out = jnp.clip(jax.random.normal(query_key, shape_full, jnp.float32) * 1.5, -9.0, 9.0)
    return (query_out, keys_out)


def draw_query_rows(key, part):
    return shared_draw(key)[0].astype(jnp.bfloat16)


def draw_key_rows(key, part):
    return shared_draw(key)[1].astype(jnp.bfloat16)


def draw_extents(key, part):
    picks = jax.random.randint(key, (HEADS, 3), 0, 2)
    values_out = 1 + 2 * picks
    chosen = jax.random.randint(jax.random.fold_in(key, 7), (), 0, HEADS)
    heads_iota = jnp.arange(HEADS)[:, None]
    values_out = jnp.where(heads_iota == chosen, 3, values_out)
    values_out = jnp.where(heads_iota == (chosen + 1) % HEADS, 1, values_out)
    return values_out.astype(jnp.int32)


def steps_of(stream_key, shape, split, smallest, high):
    level, own = 1.0, jax.random.fold_in(stream_key, 6)
    for dim, parts in split:
        draws = jnp.exp(jax.random.uniform(jax.random.fold_in(own, dim), (parts,), jnp.float32, smallest / len(split), high / len(split)))
        level = level * jnp.repeat(draws, shape[dim] // parts).reshape([-1 if axis == dim else 1 for axis in range(len(shape))])
    return level


def centred(key, shape, deviation, bound, cuts=(), kind=jnp.bfloat16):
    drawn = jax.random.normal(key, shape, jnp.float32) * deviation
    if len(cuts) > 0:
        drawn = steps_of(key, shape, cuts, -0.22, 0.18) * drawn
    return jnp.clip(drawn, min=-bound, max=bound).astype(kind)


def setup_inputs(seed: int = 0, part: int = 0) -> dict:
    arg_keys = jax.random.split(jax.random.key(seed), 5)
    part_splits = jax.random.split(jax.random.fold_in(arg_keys[4], part), 5)
    return {
        "query_rows": draw_query_rows(jax.random.fold_in(jax.random.fold_in(arg_keys[4], part), 71), part),
        "key_rows": draw_key_rows(jax.random.fold_in(jax.random.fold_in(arg_keys[4], part), 71), part),
        "value_rows": centred(part_splits[2], (TOKENS, CH), 1.0, 6.0, ((0, 16),)),
        "extents": draw_extents(jax.random.fold_in(arg_keys[4], 71), part),
    }


def reference(query_rows, key_rows, value_rows, extents):
    slab_count = N_CONTEXT
    time_tiles = slab_count // HT
    width_all = HEADS * HD
    query_slabs = query_rows.reshape(slab_count, SLAB_TOK, HEADS, HD)
    stacked = jnp.stack((key_rows, value_rows)).reshape(2, time_tiles, HT, SLAB_TOK, width_all)
    padded = jnp.pad(stacked, ((0, 0), (1, 1), (1, 1), (0, 0), (0, 0)))
    radius = (extents - 1) // 2
    positions = jnp.arange(9 * SLAB_TOK, dtype=jnp.int32)
    step_time = positions // (3 * SLAB_TOK) - 1
    step_height = positions // SLAB_TOK % 3 - 1
    key_tile = positions % SLAB_TOK // TILE_TOK
    query_tile = jnp.arange(SLAB_TOK, dtype=jnp.int32) // TILE_TOK
    width_gap = jnp.abs(query_tile[:, None] - key_tile[None, :])
    head_mask = (jnp.abs(step_time)[None, :] <= radius[:, 0:1]) & (jnp.abs(step_height)[None, :] <= radius[:, 1:2])
    width_mask = width_gap[None, :, :] <= radius[:, 2][:, None, None]
    scale_factor = 1.0 / math.sqrt(HD)

    def one_slab(slab_index):
        tile_time = slab_index // HT
        tile_height = slab_index % HT
        anchor = jnp.zeros((), jnp.int32)
        neighbourhood = lax.dynamic_slice(padded, (anchor, tile_time.astype(jnp.int32), tile_height.astype(jnp.int32), anchor, anchor), (2, 3, 3, SLAB_TOK, width_all))
        neighbourhood = neighbourhood.reshape(2, 9 * SLAB_TOK, HEADS, HD).astype(jnp.float32)
        inside = (tile_time + step_time >= 0) & (tile_time + step_time < time_tiles) & (tile_height + step_height >= 0) & (tile_height + step_height < HT)
        allowed = width_mask & head_mask[:, None, :] & inside[None, None, :]
        queries_now = query_slabs[slab_index].astype(jnp.float32)
        scores = jnp.einsum('qhd,khd->hqk', queries_now, neighbourhood[0]) * scale_factor
        masked = jnp.where(allowed, scores, jnp.float32(-1e+30))
        row_max = lax.optimization_barrier(jnp.max(masked, axis=2, keepdims=True))
        weights = jnp.exp(masked - row_max)
        totals = lax.optimization_barrier(jnp.sum(weights, axis=2, keepdims=True))
        rounded = weights.astype(jnp.bfloat16)
        mixture = jnp.einsum('hqk,khd->qhd', rounded.astype(jnp.float32), neighbourhood[1])
        mixture = mixture / jnp.transpose(totals, (1, 0, 2))
        return mixture.reshape(SLAB_TOK, width_all).astype(jnp.bfloat16)
    result = lax.map(one_slab, jnp.arange(slab_count, dtype=jnp.int32))
    return result.reshape(TOKENS, width_all)
```

```python
import functools
import math

import jax
import jax.numpy as jnp
from jax import lax
from jax.experimental import pallas as pl
from jax.experimental.pallas import tpu as pltpu
from jax.sharding import PartitionSpec as P

HEADS = 12
HD = 128
HT = 8
ROWS = 256
MASKED = -1e30
SCALE2 = math.log2(math.e) / math.sqrt(HD)
MENU = (
    (2, 1, 3), (3, 1, 4), (3, 2, 5), (4, 1, 5), (3, 3, 4), (5, 1, 5), (4, 3, 3), (6, 1, 4), (7, 1, 4), (8, 1, 2), (9, 1, 2), (12, 0, 0)
)

TALL, WIDE, TIMED, UP_OK, DOWN_OK, SIDE_OK, CHOICE = 12, 24, 36, 48, 49, 50, 52
SCHEDULE = 64
ANY = pl.BlockSpec(memory_space=pl.ANY)
VMEM = pl.BlockSpec(memory_space=pltpu.VMEM)
SMEM = pl.BlockSpec(memory_space=pltpu.SMEM)


def plan_kernel(time_tiles, extents, index, schedule):
    one, none = jnp.int32(1), jnp.int32(0)
    wide, timed, tall = [], [], []
    for head in range(HEADS):
        wide.append(jnp.where((extents[head, 2] - 1) // 2 >= 0, one, none))
        timed.append(jnp.where((extents[head, 0] - 1) // 2 >= 1, one, none))
        tall.append(jnp.where((extents[head, 1] - 1) // 2 >= 1, one, none))
    both = sum(t * h for t, h in zip(timed, tall))
    only_timed = sum(timed) - both
    only_tall = sum(tall) - both
    choice, a, b, c = (jnp.int32(x) for x in (len(MENU) - 1, *MENU[-1]))
    for place in reversed(range(len(MENU) - 1)):
        sizes = MENU[place]
        fits = both + jnp.maximum(only_timed - sizes[1], 0) + jnp.maximum(only_tall - sizes[2], 0) <= sizes[0]
        choice, a, b, c = (jnp.where(fits, jnp.int32(x), y) for x, y in zip((place, *sizes), (choice, a, b, c)))
    timed_in_a = jnp.maximum(only_timed - b, 0)
    tall_in_a = jnp.maximum(only_tall - c, 0)
    end_a = both + timed_in_a + tall_in_a
    end_b = a + only_timed - timed_in_a
    end_c = a + b + only_tall - tall_in_a
    seen = [none] * 4
    for head in range(HEADS):
        t, h = timed[head] == 1, tall[head] == 1
        rank = jnp.where(t, jnp.where(h, seen[0], seen[1]), jnp.where(h, seen[2], seen[3]))
        from_timed = jnp.where(rank < timed_in_a, both + rank, a + rank - timed_in_a)
        from_tall = jnp.where(rank < tall_in_a, both + timed_in_a + rank, a + b + rank - tall_in_a)
        left = rank - (a - end_a)
        later = left - (a + b - end_b)
        last = later - (a + b + c - end_c)
        free = jnp.where(
            left < 0, end_a + rank, jnp.where(later < 0, end_b + left, jnp.where(last < 0, end_c + later, a + b + c + last))
        )
        place = jnp.where(t, jnp.where(h, rank, from_timed), jnp.where(h, from_tall, free))
        for kind, is_kind in enumerate((t & h, t & ~h, ~t & h, ~t & ~h)):
            seen[kind] = seen[kind] + jnp.where(is_kind, one, none)
        schedule[place] = jnp.int32(head)
        schedule[TALL + place] = tall[head]
        schedule[WIDE + place] = wide[head]
        schedule[TIMED + place] = timed[head]
    time_index, height_index = lax.div(index[0], jnp.int32(HT)), lax.rem(index[0], jnp.int32(HT))
    schedule[UP_OK] = jnp.where(height_index > 0, one, none)
    schedule[DOWN_OK] = jnp.where(height_index < HT - 1, one, none)
    schedule[SIDE_OK] = jnp.where(time_index > 0, one, none)
    schedule[SIDE_OK + 1] = jnp.where(time_index < time_tiles - 1, one, none)
    schedule[CHOICE] = choice
    for place in range(CHOICE + 1, SCHEDULE):
        schedule[place] = none


def plan(extents, index, time_tiles):
    return pl.pallas_call(
        functools.partial(plan_kernel, time_tiles),
        out_shape=jax.ShapeDtypeStruct((SCHEDULE,), jnp.int32),
        in_specs=[SMEM, SMEM],
        out_specs=SMEM,
        name="plan",
    )(extents, index)


def each(count, body):
    def one(place, carry):
        body(place)
        return carry

    if count > 1:
        lax.fori_loop(0, count, one, 0)
    elif count:
        body(0)


def levels_of(a):
    return -(-a // 8) * 8


def columns(schedule, place):
    return pl.ds(pl.multiple_of(schedule[place] * HD, HD), HD)


def call(kernel, schedule, operands, outs, scratch=(), specs=None, out_specs=None, aliases=None, cost=None, name=None):
    return pl.pallas_call(
        kernel,
        out_shape=outs,
        grid_spec=pltpu.PrefetchScalarGridSpec(
            num_scalar_prefetch=1,
            in_specs=specs or [VMEM] * len(operands),
            out_specs=out_specs or [VMEM] * len(outs),
            scratch_shapes=list(scratch),
        ),
        input_output_aliases=aliases or {},
        compiler_params=pltpu.CompilerParams(vmem_limit_bytes=40 * 2**20),
        cost_estimate=cost,
        name=name,
    )(schedule, *operands)


def cost_of(slabs, arrays):
    return pl.CostEstimate(
        flops=slabs * 4 * ROWS * ROWS * HD * 4, bytes_accessed=arrays * ROWS * HD * 2, transcendentals=slabs * ROWS * ROWS
    )


def pack_kernel(firsts, sources, schedule, *refs):
    inputs, outs, sems = refs[:sources], refs[sources:-1], refs[-1]

    def copies(act):
        for first, out in zip(firsts, outs):
            for which, source in enumerate(inputs):

                def one(place):
                    target = out.at[place] if sources == 1 else out.at[which, place]
                    act(pltpu.make_async_copy(source.at[:, columns(schedule, first + place)], target, sems.at[first + place, which]))

                each(out.shape[-3], one)

    copies(lambda copy: copy.start())
    copies(lambda copy: copy.wait())


def pack(schedule, sources, pieces):
    lead = () if len(sources) == 1 else (len(sources),)
    pieces = [(first, size) for first, size in pieces if size]
    return call(
        functools.partial(pack_kernel, [first for first, _ in pieces], len(sources)),
        schedule,
        sources,
        [jax.ShapeDtypeStruct((*lead, size, ROWS, HD), sources[0].dtype) for _, size in pieces],
        scratch=[pltpu.SemaphoreType.DMA((HEADS, len(sources)))],
        specs=[ANY] * len(sources),
        cost=cost_of(0, 8 * len(sources)),
        name="pack",
    )


def attend(query, slabs):
    scores, tops = [], []
    for key, _, ok in slabs:
        score = lax.dot_general(key, query, (((1,), (1,)), ((), ())), preferred_element_type=jnp.float32)
        scores.append(score)
        tops.append(jnp.where(ok, jnp.max(score, axis=0, keepdims=True), jnp.float32(MASKED)))
    top = functools.reduce(jnp.maximum, tops)
    total, mixture = None, None
    for score, (_, value, ok) in zip(scores, slabs):
        weight = jnp.exp2((score - jnp.where(ok, top, jnp.float32(-MASKED))) * SCALE2)
        part = jnp.sum(weight, axis=0, keepdims=True)
        mixed = lax.dot_general(
            value, weight.astype(jnp.bfloat16), (((0,), (0,)), ((), ())), preferred_element_type=jnp.float32
        )
        total = part if total is None else total + part
        mixture = mixed if mixture is None else mixture + mixed
    return mixture * (1.0 / total), top * SCALE2 + jnp.log2(total)


def own_slab(schedule, place, k, v):
    at = columns(schedule, place)
    return k[:, at], v[:, at], schedule[WIDE + place] == 1


def tall_slabs(schedule, place, slot, up, down):
    tall = schedule[TALL + place]
    return [
        (up[0, slot], up[1, slot], tall * schedule[UP_OK] == 1),
        (down[0, slot], down[1, slot], tall * schedule[DOWN_OK] == 1),
    ]


def partial_kernel(schedule, q, k, v, up, down, out, levels):
    a = q.shape[0]
    rows = levels.shape[0]
    levels[...] = jnp.zeros_like(levels)

    def body(place):
        slabs = [own_slab(schedule, place, k, v)] + tall_slabs(schedule, place, place, up, down)
        mixture, level = attend(q[place], slabs)
        out[pl.ds(pl.multiple_of(place * HD, HD), HD), :] = mixture.astype(out.dtype)
        levels[pl.ds(place, 1), :] = level

    each(a, body)
    level = levels[...]
    pieces = []
    for _ in range(3):
        piece = level.astype(jnp.bfloat16)
        level = level - piece.astype(jnp.float32)
        pieces.append(piece)
    for place, piece in enumerate(pieces):
        out[pl.ds(a * HD + place * rows, rows), :] = piece


def partial_attention(schedule, q, k, v, up, down):
    a = q.shape[0]
    return call(
        partial_kernel,
        schedule,
        [q, k, v, up, down],
        [jax.ShapeDtypeStruct((a * HD + 3 * levels_of(a), ROWS), jnp.bfloat16)],
        scratch=[pltpu.VMEM((levels_of(a), ROWS), jnp.float32)],
        cost=cost_of(3 * a, 24 + 6 * a),
        name="partial_attention",
    )[0]


def local_kernel(a, timed, c, schedule, q, k, v, up, down, *refs):
    if c:
        up2, down2, *refs = refs
    out, mix, stat = refs

    def with_time(place):
        slabs = [own_slab(schedule, place, k, v)] + tall_slabs(schedule, place, place, up, down)
        mixture, level = attend(q[:, columns(schedule, place)], slabs)
        mix[place] = mixture
        stat[pl.ds(place, 1), :] = level

    def with_height(slot):
        place = timed + slot
        slabs = [own_slab(schedule, place, k, v)] + tall_slabs(schedule, place, slot, up2, down2)
        mixture, _ = attend(q[:, columns(schedule, place)], slabs)
        out[:, columns(schedule, place)] = mixture.T.astype(out.dtype)

    def alone(slot):
        place = timed + c + slot
        mixture, _ = attend(q[:, columns(schedule, place)], [own_slab(schedule, place, k, v)])
        out[:, columns(schedule, place)] = mixture.T.astype(out.dtype)

    each(a, with_time)
    each(c, with_height)
    each(HEADS - timed - c, alone)


def local_attention(schedule, q, k, v, ups, downs, a, timed, c):
    operands = [q, k, v, ups[0], downs[0]] + ([ups[1], downs[1]] if c else [])
    return call(
        functools.partial(local_kernel, a, timed, c),
        schedule,
        operands,
        [
            jax.ShapeDtypeStruct(q.shape, jnp.bfloat16),
            jax.ShapeDtypeStruct((a, HD, ROWS), jnp.float32),
            jax.ShapeDtypeStruct((levels_of(a), ROWS), jnp.float32),
        ],
        cost=cost_of(3 * (a + c) + HEADS - timed - c, 48 + 8 * a),
        name="local_attention",
    )


def store_columns(schedule, first, count, out, result, sems, body):
    def one(slot):
        result[slot] = body(slot).astype(result.dtype)
        pltpu.make_async_copy(result.at[slot], out.at[:, columns(schedule, first + slot)], sems.at[slot]).start()

    def done(slot):
        pltpu.make_async_copy(result.at[slot], out.at[:, columns(schedule, first + slot)], sems.at[slot]).wait()

    each(count, one)
    each(count, done)


def side_ok(schedule, place, side):
    timed = schedule[TIMED + place]
    return (timed if side is None else timed * schedule[SIDE_OK + side]) == 1


def timed_kernel(a, sides, schedule, q, k, v, *refs):
    parts = refs[: len(sides)]
    out, result, sems = refs[-3:]

    def body(slot):
        place = a + slot
        slabs = [own_slab(schedule, place, k, v)]
        for side, part in zip(sides, parts):
            slabs.append((part[0, slot], part[1, slot], side_ok(schedule, place, side)))
        return attend(q[:, columns(schedule, place)], slabs)[0].T

    store_columns(schedule, a, result.shape[0], out, result, sems, body)


def combine_kernel(sides, schedule, mix, stat, *refs):
    parts = refs[: len(sides)]
    out, result, sems, levels = refs[-4:]
    a, rows = mix.shape[0], stat.shape[0]
    for which, part in enumerate(parts):
        levels[which] = sum(part[pl.ds(a * HD + place * rows, rows), :].astype(jnp.float32) for place in range(3))

    def body(slot):
        every, mixtures = [stat[pl.ds(slot, 1), :]], [mix[slot]]
        for which, (side, part) in enumerate(zip(sides, parts)):
            level = levels[which, pl.ds(slot, 1), :]
            every.append(jnp.where(side_ok(schedule, slot, side), level, jnp.float32(MASKED)))
            mixtures.append(part[pl.ds(pl.multiple_of(slot * HD, HD), HD), :].astype(jnp.float32))
        top = functools.reduce(jnp.maximum, every)
        shares = [jnp.exp2(level - top) for level in every]
        inverse = 1.0 / functools.reduce(jnp.add, shares)
        return functools.reduce(jnp.add, [(share * inverse) * mixture for share, mixture in zip(shares, mixtures)]).T

    store_columns(schedule, 0, a, out, result, sems, body)


def into_columns(kernel, schedule, operands, out, count, scratch, cost, name):
    return call(
        kernel,
        schedule,
        [*operands, out],
        [jax.ShapeDtypeStruct(out.shape, out.dtype)],
        scratch=[pltpu.VMEM((count, ROWS, HD), jnp.bfloat16), pltpu.SemaphoreType.DMA((count,)), *scratch],
        specs=[VMEM] * len(operands) + [ANY],
        out_specs=[ANY],
        aliases={1 + len(operands): 0},
        cost=cost,
        name=name,
    )[0]


def after(value, *earlier):
    return lax.optimization_barrier((value, *earlier))[0]


def branch(a, b, c, time_tiles, q, k, v, schedule):
    count = time_tiles * HT
    if time_tiles == 2:
        routes = [[(i, (i + HT) % count) for i in range(count)]]
        sides = [None]
    else:
        routes = [[(i, i + HT) for i in range(count - HT)], [(i + HT, i) for i in range(count - HT)]]
        sides = [0, 1]
    backs = [[(there, here) for here, there in route] for route in routes]
    upward = [(i, i + 1) for i in range(count - 1) if i % HT != HT - 1]
    downward = [(there, here) for here, there in upward]

    def move(value, pairs):
        return lax.ppermute(value, "context", pairs)

    (queries,) = pack(schedule, [q], [(0, a)])
    sent = [move(queries, route) for route in routes]
    pieces = list(pack(schedule, after([k, v], queries), [(0, a), (a, b), (a + b, c)]))
    near = pieces.pop(0)
    across = pieces.pop(0) if b else None
    later = pieces.pop(0) if c else None
    ups, downs = [move(near, upward)], [move(near, downward)]
    if b:
        across = after(across, *sent)
        others = [move(across, pairs) for pairs in routes]
    if c:
        later = after(later, *sent)
        ups.append(move(later, upward))
        downs.append(move(later, downward))
    parts = [move(partial_attention(schedule, query, k, v, ups[0], downs[0]), back) for query, back in zip(sent, backs)]
    out, mix, stat = local_attention(schedule, q, k, v, ups, downs, a, a + b, c)
    if b:
        out = into_columns(
            functools.partial(timed_kernel, a, sides), schedule, [q, k, v, *others], out, b, [], cost_of(2 * b, 24 + 4 * b), "timed"
        )
    scratch = [pltpu.VMEM((len(sides), levels_of(a), ROWS), jnp.float32)]
    return into_columns(
        functools.partial(combine_kernel, sides[::-1]), schedule, [mix, stat, *parts], out, a, scratch, cost_of(0, 8 * a), "combine"
    )


def local(query_rows, key_rows, value_rows, extents):
    time_tiles = lax.axis_size("context") // HT
    index = lax.axis_index("context").astype(jnp.int32).reshape(1)
    schedule = plan(extents, index, time_tiles)
    branches = [functools.partial(branch, *sizes, time_tiles) for sizes in MENU]
    return lax.switch(schedule[CHOICE], branches, query_rows, key_rows, value_rows, schedule)


def solution(mesh):
    placed = P(("groups", "context"), None)
    return jax.shard_map(local, mesh=mesh, in_specs=(placed, placed, placed, P()), out_specs=placed, check_vma=False)
```

```python
import functools
import math

import jax
import jax.numpy as jnp
from jax import lax
from jax.experimental import pallas as pl
from jax.experimental.pallas import tpu as pltpu
from jax.sharding import PartitionSpec as P

HEADS = 12
HD = 128
HT = 8
ROWS = 256
MASKED = -1e30
SCALE2 = math.log2(math.e) / math.sqrt(HD)
PACK_LIMIT = 62
UNIT = 6 * 10**8
MENU = ((3, 1, 4), (3, 2, 5), (4, 1, 5), (4, 2, 4), (5, 1, 5), (5, 2, 4), (6, 2, 3), (7, 2, 3), (12, 0, 0))

TALL, WIDE, TIMED, UP_OK, DOWN_OK, SIDE_OK = 12, 24, 36, 48, 49, 50
SCHEDULE = 64
ANY = pl.BlockSpec(memory_space=pl.ANY)
VMEM = pl.BlockSpec(memory_space=pltpu.VMEM)
SMEM = pl.BlockSpec(memory_space=pltpu.SMEM)


def plan_kernel(time_tiles, extents, index, schedule, chosen):
    one, none = jnp.int32(1), jnp.int32(0)
    wide, timed, tall = [], [], []
    for head in range(HEADS):
        wide.append(jnp.where((extents[2, head] - 1) // 2 >= 0, one, none))
        timed.append(jnp.where((extents[0, head] - 1) // 2 >= 1, one, none))
        tall.append(jnp.where((extents[1, head] - 1) // 2 >= 1, one, none))
    both = sum(t * h for t, h in zip(timed, tall))
    only_timed = sum(timed) - both
    only_tall = sum(tall) - both
    choice, a, b, c = (jnp.int32(x) for x in (len(MENU) - 1, *MENU[-1]))
    for place in reversed(range(len(MENU) - 1)):
        sizes = MENU[place]
        fits = both + jnp.maximum(only_timed - sizes[1], 0) + jnp.maximum(only_tall - sizes[2], 0) <= sizes[0]
        choice, a, b, c = (jnp.where(fits, jnp.int32(x), y) for x, y in zip((place, *sizes), (choice, a, b, c)))
    timed_in_a = jnp.maximum(only_timed - b, 0)
    tall_in_a = jnp.maximum(only_tall - c, 0)
    end_a = both + timed_in_a + tall_in_a
    end_b = a + only_timed - timed_in_a
    end_c = a + b + only_tall - tall_in_a
    seen = [none] * 4
    for head in range(HEADS):
        t, h = timed[head] == 1, tall[head] == 1
        rank = jnp.where(t, jnp.where(h, seen[0], seen[1]), jnp.where(h, seen[2], seen[3]))
        from_timed = jnp.where(rank < timed_in_a, both + rank, a + rank - timed_in_a)
        from_tall = jnp.where(rank < tall_in_a, both + timed_in_a + rank, a + b + rank - tall_in_a)
        left = rank - (a - end_a)
        later = left - (a + b - end_b)
        last = later - (a + b + c - end_c)
        free = jnp.where(
            left < 0, end_a + rank, jnp.where(later < 0, end_b + left, jnp.where(last < 0, end_c + later, a + b + c + last))
        )
        place = jnp.where(t, jnp.where(h, rank, from_timed), jnp.where(h, from_tall, free))
        for kind, is_kind in enumerate((t & h, t & ~h, ~t & h, ~t & ~h)):
            seen[kind] = seen[kind] + jnp.where(is_kind, one, none)
        schedule[place] = jnp.int32(head)
        schedule[TALL + place] = tall[head]
        schedule[WIDE + place] = wide[head]
        schedule[TIMED + place] = timed[head]
    time_index, height_index = lax.div(index[0], jnp.int32(HT)), lax.rem(index[0], jnp.int32(HT))
    schedule[UP_OK] = jnp.where(height_index > 0, one, none)
    schedule[DOWN_OK] = jnp.where(height_index < HT - 1, one, none)
    schedule[SIDE_OK] = jnp.where(time_index > 0, one, none)
    schedule[SIDE_OK + 1] = jnp.where(time_index < time_tiles - 1, one, none)
    chosen[0] = choice
    for place in range(SIDE_OK + 2, SCHEDULE):
        schedule[place] = none


def plan(extents, index, time_tiles):
    return pl.pallas_call(
        functools.partial(plan_kernel, time_tiles),
        out_shape=[jax.ShapeDtypeStruct((SCHEDULE,), jnp.int32), jax.ShapeDtypeStruct((1,), jnp.int32)],
        in_specs=[SMEM, SMEM],
        out_specs=[SMEM, SMEM],
        name="plan",
    )(extents.T, index)


def each(count, body):
    def one(place, carry):
        body(place)
        return carry

    if count > 1:
        lax.fori_loop(0, count, one, 0)
    elif count:
        body(0)


def levels_of(a):
    return -(-a // 8) * 8


def columns(schedule, place):
    return pl.ds(pl.multiple_of(schedule[place] * HD, HD), HD)


def call(kernel, schedule, operands, outs, scratch=(), specs=None, out_specs=None, aliases=None, cost=None, name=None, limit=40):
    return pl.pallas_call(
        kernel,
        out_shape=outs,
        grid_spec=pltpu.PrefetchScalarGridSpec(
            num_scalar_prefetch=1,
            in_specs=specs or [VMEM] * len(operands),
            out_specs=out_specs or [VMEM] * len(outs),
            scratch_shapes=list(scratch),
        ),
        input_output_aliases=aliases or {},
        compiler_params=pltpu.CompilerParams(vmem_limit_bytes=limit * 2**20),
        cost_estimate=cost,
        name=name,
    )(schedule, *operands)


LONG = pl.CostEstimate(flops=10**11, bytes_accessed=10**6, transcendentals=0)
SHORT = pl.CostEstimate(flops=10**6, bytes_accessed=10**5, transcendentals=0)


def waiting(units):
    return pl.CostEstimate(flops=int(max(units, 0) * UNIT), bytes_accessed=10**5, transcendentals=0)


def pack_kernel(firsts, sources, apart, schedule, *refs):
    inputs, outs, sems = refs[:sources], list(refs[sources:-1]), refs[-1]
    if apart:
        outs[:sources] = [outs[:sources]]

    def copies(act):
        for first, out in zip(firsts, outs):
            for which, source in enumerate(inputs):
                target = out[which] if isinstance(out, list) else out.at[which]

                def one(place):
                    at = columns(schedule, first + place)
                    act(pltpu.make_async_copy(source.at[:, at], target.at[place], sems.at[first + place, which]))

                each(target.shape[0], one)

    copies(lambda copy: copy.start())
    copies(lambda copy: copy.wait())


def pack(schedule, sources, pieces, apart, limit=40):
    pieces = [(first, size) for first, size in pieces if size]
    shapes = [(len(sources), size, ROWS, HD) for _, size in pieces]
    if apart:
        shapes[:1] = [shapes[0][1:]] * len(sources)
    return list(call(
        functools.partial(pack_kernel, [first for first, _ in pieces], len(sources), apart),
        schedule,
        sources,
        [jax.ShapeDtypeStruct(shape, sources[0].dtype) for shape in shapes],
        scratch=[pltpu.SemaphoreType.DMA((HEADS, len(sources)))],
        specs=[ANY] * len(sources),
        cost=SHORT,
        name="pack",
        limit=limit,
    ))


def attend(query, slabs):
    scores, tops = [], []
    for key, _, ok in slabs:
        score = lax.dot_general(key, query, (((1,), (1,)), ((), ())), preferred_element_type=jnp.float32)
        scores.append(score)
        tops.append(jnp.where(ok, jnp.max(score, axis=0, keepdims=True), jnp.float32(MASKED)))
    top = functools.reduce(jnp.maximum, tops)
    total, mixture = None, None
    for score, (_, value, ok) in zip(scores, slabs):
        weight = jnp.exp2((score - jnp.where(ok, top, jnp.float32(-MASKED))) * SCALE2)
        part = jnp.sum(weight, axis=0, keepdims=True)
        mixed = lax.dot_general(
            value, weight.astype(jnp.bfloat16), (((0,), (0,)), ((), ())), preferred_element_type=jnp.float32
        )
        total = part if total is None else total + part
        mixture = mixed if mixture is None else mixture + mixed
    return mixture * (1.0 / total), top * SCALE2 + jnp.log2(total)


def own_slab(schedule, place, k, v):
    at = columns(schedule, place)
    return k[:, at], v[:, at], schedule[WIDE + place] == 1


def tall_slabs(schedule, place, slot, heights):
    tall = schedule[TALL + place]
    if len(heights) == 2:
        heights = [piece.at[which] for piece in heights for which in range(2)]
    return [
        (heights[0][slot], heights[1][slot], tall * schedule[UP_OK] == 1),
        (heights[2][slot], heights[3][slot], tall * schedule[DOWN_OK] == 1),
    ]


def partial_kernel(schedule, q, k, v, *refs):
    heights, (out, levels) = refs[:-2], refs[-2:]
    a = q.shape[0]
    rows = levels.shape[0]
    levels[...] = jnp.zeros_like(levels)

    def body(place):
        slabs = [own_slab(schedule, place, k, v)] + tall_slabs(schedule, place, place, heights)
        mixture, level = attend(q[place], slabs)
        out[pl.ds(pl.multiple_of(place * HD, HD), HD), :] = mixture.astype(out.dtype)
        levels[pl.ds(place, 1), :] = level

    each(a, body)
    level = levels[...]
    pieces = []
    for _ in range(3):
        piece = level.astype(jnp.bfloat16)
        level = level - piece.astype(jnp.float32)
        pieces.append(piece)
    for place, piece in enumerate(pieces):
        out[pl.ds(a * HD + place * rows, rows), :] = piece


def partial_attention(schedule, q, k, v, heights):
    a = q.shape[0]
    return call(
        partial_kernel,
        schedule,
        [q, k, v, *heights],
        [jax.ShapeDtypeStruct((a * HD + 3 * levels_of(a), ROWS), jnp.bfloat16)],
        scratch=[pltpu.VMEM((levels_of(a), ROWS), jnp.float32)],
        cost=SHORT,
        name="partial_attention",
    )[0]


def local_kernel(a, late, schedule, q, k, v, *refs):
    heights, (out, mix, stat) = refs[:-3], refs[-3:]

    def with_time(place):
        slabs = [own_slab(schedule, place, k, v)] + tall_slabs(schedule, place, place, heights)
        mixture, level = attend(q[:, columns(schedule, place)], slabs)
        mix[place] = mixture
        stat[pl.ds(place, 1), :] = level

    def alone(slot):
        place = late + slot
        mixture, _ = attend(q[:, columns(schedule, place)], [own_slab(schedule, place, k, v)])
        out[:, columns(schedule, place)] = mixture.T.astype(out.dtype)

    each(a, with_time)
    each(HEADS - late, alone)


def local_attention(schedule, q, k, v, heights, a, late):
    return call(
        functools.partial(local_kernel, a, late),
        schedule,
        [q, k, v, *heights],
        [
            jax.ShapeDtypeStruct(q.shape, jnp.bfloat16),
            jax.ShapeDtypeStruct((a, HD, ROWS), jnp.float32),
            jax.ShapeDtypeStruct((levels_of(a), ROWS), jnp.float32),
        ],
        cost=SHORT,
        name="local_attention",
    )


def store_columns(schedule, first, count, out, result, sems, body):
    def one(slot):
        result[slot] = body(slot).astype(result.dtype)
        pltpu.make_async_copy(result.at[slot], out.at[:, columns(schedule, first + slot)], sems.at[slot]).start()

    def done(slot):
        pltpu.make_async_copy(result.at[slot], out.at[:, columns(schedule, first + slot)], sems.at[slot]).wait()

    each(count, one)
    each(count, done)


def side_ok(schedule, place, side):
    timed = schedule[TIMED + place]
    return (timed if side is None else timed * schedule[SIDE_OK + side]) == 1


def timed_kernel(a, sides, schedule, q, k, v, *refs):
    parts = refs[: len(sides)]
    out, result, sems = refs[-3:]

    def body(slot):
        place = a + slot
        slabs = [own_slab(schedule, place, k, v)]
        for side, part in zip(sides, parts):
            slabs.append((part[0, slot], part[1, slot], side_ok(schedule, place, side)))
        return attend(q[:, columns(schedule, place)], slabs)[0].T

    store_columns(schedule, a, result.shape[0], out, result, sems, body)


def tall_kernel(first, schedule, q, k, v, up, down, _, out, result, sems):
    def body(slot):
        place = first + slot
        slabs = [own_slab(schedule, place, k, v)] + tall_slabs(schedule, place, slot, [up, down])
        return attend(q[:, columns(schedule, place)], slabs)[0].T

    store_columns(schedule, first, result.shape[0], out, result, sems, body)


def combine_kernel(sides, schedule, mix, stat, *refs):
    parts = refs[: len(sides)]
    out, result, sems, levels = refs[-4:]
    a, rows = mix.shape[0], stat.shape[0]
    for which, part in enumerate(parts):
        levels[which] = sum(part[pl.ds(a * HD + place * rows, rows), :].astype(jnp.float32) for place in range(3))

    def body(slot):
        every, mixtures = [stat[pl.ds(slot, 1), :]], [mix[slot]]
        for which, (side, part) in enumerate(zip(sides, parts)):
            level = levels[which, pl.ds(slot, 1), :]
            every.append(jnp.where(side_ok(schedule, slot, side), level, jnp.float32(MASKED)))
            mixtures.append(part[pl.ds(pl.multiple_of(slot * HD, HD), HD), :].astype(jnp.float32))
        top = functools.reduce(jnp.maximum, every)
        shares = [jnp.exp2(level - top) for level in every]
        inverse = 1.0 / functools.reduce(jnp.add, shares)
        return functools.reduce(jnp.add, [(share * inverse) * mixture for share, mixture in zip(shares, mixtures)]).T

    store_columns(schedule, 0, a, out, result, sems, body)


def into_columns(kernel, schedule, operands, out, count, scratch, cost, name):
    return call(
        kernel,
        schedule,
        [*operands, out],
        [jax.ShapeDtypeStruct(out.shape, out.dtype)],
        scratch=[pltpu.VMEM((count, ROWS, HD), jnp.bfloat16), pltpu.SemaphoreType.DMA((count,)), *scratch],
        specs=[VMEM] * len(operands) + [ANY],
        out_specs=[ANY],
        aliases={1 + len(operands): 0},
        cost=cost,
        name=name,
    )[0]


def after(value, *earlier):
    return lax.optimization_barrier((value, *earlier))[0]


def branch(a, b, c, time_tiles, q, k, v, schedule):
    count = time_tiles * HT
    if time_tiles == 2:
        routes = [[(i, (i + HT) % count) for i in range(count)]]
        sides = [None]
    else:
        routes = [[(i, i + HT) for i in range(count - HT)], [(i + HT, i) for i in range(count - HT)]]
        sides = [0, 1]
    backs = [[(there, here) for here, there in route] for route in routes]
    upward = [(i, i + 1) for i in range(count - 1) if i % HT != HT - 1]
    downward = [(there, here) for here, there in upward]

    def move(value, pairs):
        return lax.ppermute(value, "context", pairs)

    apart = a >= 2 * b
    (queries,) = pack(schedule, [q], [(0, a)], True, PACK_LIMIT)
    sent = [move(queries, route) for route in routes]
    pieces = pack(schedule, after([k, v], queries), [(0, a), (a, b), (a + b, c)], apart)
    nears = [pieces.pop(0) for _ in range(2 if apart else 1)]
    across = pieces.pop(0) if b else None
    later = pieces.pop(0) if c else None
    near = [move(piece, pairs) for pairs in (upward, downward) for piece in nears]
    if b:
        across = after(across, *sent)
        others = [move(across, pairs) for pairs in routes]
    parts = [partial_attention(schedule, query, k, v, near) for query in sent]
    if c:
        later = after(later, *sent)
        heights = [move(later, upward), move(later, downward)]
    parts = [move(part, back) for part, back in zip(parts, backs)]
    out, mix, stat = local_attention(schedule, q, k, v, near, a, a + b + c)
    if b:
        kernel = functools.partial(timed_kernel, a, sides)
        out = into_columns(kernel, schedule, [q, k, v, *others], out, b, [], waiting(2 * c - b), "timed")
    if c:
        kernel = functools.partial(tall_kernel, a + b)
        out = into_columns(kernel, schedule, [q, k, v, *heights], out, c, [], LONG, "tall")
    scratch = [pltpu.VMEM((len(sides), levels_of(a), ROWS), jnp.float32)]
    return into_columns(
        functools.partial(combine_kernel, sides[::-1]), schedule, [mix, stat, *parts], out, a, scratch, LONG, "combine"
    )


def local(query_rows, key_rows, value_rows, extents):
    time_tiles = lax.axis_size("context") // HT
    index = lax.axis_index("context").astype(jnp.int32).reshape(1)
    schedule, choice = plan(extents, index, time_tiles)
    branches = [functools.partial(branch, *sizes, time_tiles) for sizes in MENU]
    return lax.switch(choice.reshape(()), branches, query_rows, key_rows, value_rows, schedule)


def solution(mesh):
    placed = P(("groups", "context"), None)
    return jax.shard_map(local, mesh=mesh, in_specs=(placed, placed, placed, P()), out_specs=placed, check_vma=False)
```

```python
import functools
import math

import jax
import jax.numpy as jnp
from jax import lax
from jax.experimental import pallas as pl
from jax.experimental.pallas import tpu as pltpu
from jax.sharding import PartitionSpec as P

HEADS = 12
HD = 128
HT = 8
ROWS = 256
MASKED = -1e30
SCALE2 = math.log2(math.e) / math.sqrt(HD)
PACK_LIMIT = 62
FILL = 8e9
WAIT = 8e9
MENU = ((3, 1, 4), (3, 2, 5), (4, 1, 5), (4, 2, 4), (5, 1, 5), (5, 2, 4), (6, 2, 3), (7, 2, 3), (12, 0, 0))

TALL, WIDE, TIMED, UP_OK, DOWN_OK, SIDE_OK = 12, 24, 36, 48, 49, 50
SCHEDULE = 64
ANY = pl.BlockSpec(memory_space=pl.ANY)
VMEM = pl.BlockSpec(memory_space=pltpu.VMEM)
SMEM = pl.BlockSpec(memory_space=pltpu.SMEM)


def plan_kernel(time_tiles, extents, index, schedule, chosen):
    one, none = jnp.int32(1), jnp.int32(0)
    wide, timed, tall = [], [], []
    for head in range(HEADS):
        wide.append(jnp.where((extents[2, head] - 1) // 2 >= 0, one, none))
        timed.append(jnp.where((extents[0, head] - 1) // 2 >= 1, one, none))
        tall.append(jnp.where((extents[1, head] - 1) // 2 >= 1, one, none))
    both = sum(t * h for t, h in zip(timed, tall))
    only_timed = sum(timed) - both
    only_tall = sum(tall) - both
    choice, a, b, c = (jnp.int32(x) for x in (len(MENU) - 1, *MENU[-1]))
    for place in reversed(range(len(MENU) - 1)):
        sizes = MENU[place]
        fits = both + jnp.maximum(only_timed - sizes[1], 0) + jnp.maximum(only_tall - sizes[2], 0) <= sizes[0]
        choice, a, b, c = (jnp.where(fits, jnp.int32(x), y) for x, y in zip((place, *sizes), (choice, a, b, c)))
    timed_in_a = jnp.maximum(only_timed - b, 0)
    tall_in_a = jnp.maximum(only_tall - c, 0)
    end_a = both + timed_in_a + tall_in_a
    end_b = a + only_timed - timed_in_a
    end_c = a + b + only_tall - tall_in_a
    seen = [none] * 4
    for head in range(HEADS):
        t, h = timed[head] == 1, tall[head] == 1
        rank = jnp.where(t, jnp.where(h, seen[0], seen[1]), jnp.where(h, seen[2], seen[3]))
        from_timed = jnp.where(rank < timed_in_a, both + rank, a + rank - timed_in_a)
        from_tall = jnp.where(rank < tall_in_a, both + timed_in_a + rank, a + b + rank - tall_in_a)
        left = rank - (a - end_a)
        later = left - (a + b - end_b)
        last = later - (a + b + c - end_c)
        free = jnp.where(
            left < 0, end_a + rank, jnp.where(later < 0, end_b + left, jnp.where(last < 0, end_c + later, a + b + c + last))
        )
        place = jnp.where(t, jnp.where(h, rank, from_timed), jnp.where(h, from_tall, free))
        for kind, is_kind in enumerate((t & h, t & ~h, ~t & h, ~t & ~h)):
            seen[kind] = seen[kind] + jnp.where(is_kind, one, none)
        schedule[place] = jnp.int32(head)
        schedule[TALL + place] = tall[head]
        schedule[WIDE + place] = wide[head]
        schedule[TIMED + place] = timed[head]
    time_index, height_index = lax.div(index[0], jnp.int32(HT)), lax.rem(index[0], jnp.int32(HT))
    schedule[UP_OK] = jnp.where(height_index > 0, one, none)
    schedule[DOWN_OK] = jnp.where(height_index < HT - 1, one, none)
    schedule[SIDE_OK] = jnp.where(time_index > 0, one, none)
    schedule[SIDE_OK + 1] = jnp.where(time_index < time_tiles - 1, one, none)
    chosen[0] = choice
    for place in range(SIDE_OK + 2, SCHEDULE):
        schedule[place] = none


def plan(extents, index, time_tiles):
    return pl.pallas_call(
        functools.partial(plan_kernel, time_tiles),
        out_shape=[jax.ShapeDtypeStruct((SCHEDULE,), jnp.int32), jax.ShapeDtypeStruct((1,), jnp.int32)],
        in_specs=[SMEM, SMEM],
        out_specs=[SMEM, SMEM],
        name="plan",
    )(extents.T, index)


def each(count, body):
    def one(place, carry):
        body(place)
        return carry

    if count > 1:
        lax.fori_loop(0, count, one, 0)
    elif count:
        body(0)


def levels_of(a):
    return -(-a // 8) * 8


def columns(schedule, place):
    return pl.ds(pl.multiple_of(schedule[place] * HD, HD), HD)


def call(kernel, schedule, operands, outs, scratch=(), specs=None, out_specs=None, aliases=None, cost=None, name=None, limit=40):
    return pl.pallas_call(
        kernel,
        out_shape=outs,
        grid_spec=pltpu.PrefetchScalarGridSpec(
            num_scalar_prefetch=1,
            in_specs=specs or [VMEM] * len(operands),
            out_specs=out_specs or [VMEM] * len(outs),
            scratch_shapes=list(scratch),
        ),
        input_output_aliases=aliases or {},
        compiler_params=pltpu.CompilerParams(vmem_limit_bytes=limit * 2**20),
        cost_estimate=cost,
        name=name,
    )(schedule, *operands)


LONG = pl.CostEstimate(flops=10**11, bytes_accessed=10**6, transcendentals=0)
SHORT = pl.CostEstimate(flops=10**6, bytes_accessed=10**5, transcendentals=0)


def hint(flops):
    return pl.CostEstimate(flops=int(flops), bytes_accessed=10**5, transcendentals=0)


def pack_kernel(firsts, sources, apart, schedule, *refs):
    inputs, outs, sems = refs[:sources], list(refs[sources:-1]), refs[-1]
    if apart:
        outs[:sources] = [outs[:sources]]

    def copies(act):
        for first, out in zip(firsts, outs):
            for which, source in enumerate(inputs):
                target = out[which] if isinstance(out, list) else out.at[which]

                def one(place):
                    at = columns(schedule, first + place)
                    act(pltpu.make_async_copy(source.at[:, at], target.at[place], sems.at[first + place, which]))

                each(target.shape[0], one)

    copies(lambda copy: copy.start())
    copies(lambda copy: copy.wait())


def pack(schedule, sources, pieces, apart, limit=40):
    pieces = [(first, size) for first, size in pieces if size]
    shapes = [(len(sources), size, ROWS, HD) for _, size in pieces]
    if apart:
        shapes[:1] = [shapes[0][1:]] * len(sources)
    return list(call(
        functools.partial(pack_kernel, [first for first, _ in pieces], len(sources), apart),
        schedule,
        sources,
        [jax.ShapeDtypeStruct(shape, sources[0].dtype) for shape in shapes],
        scratch=[pltpu.SemaphoreType.DMA((HEADS, len(sources)))],
        specs=[ANY] * len(sources),
        cost=SHORT,
        name="pack",
        limit=limit,
    ))


def attend(query, slabs):
    scores, tops = [], []
    for key, _, ok in slabs:
        score = lax.dot_general(key, query, (((1,), (1,)), ((), ())), preferred_element_type=jnp.float32)
        scores.append(score)
        tops.append(jnp.where(ok, jnp.max(score, axis=0, keepdims=True), jnp.float32(MASKED)))
    top = functools.reduce(jnp.maximum, tops)
    total, mixture = None, None
    for score, (_, value, ok) in zip(scores, slabs):
        weight = jnp.exp2((score - jnp.where(ok, top, jnp.float32(-MASKED))) * SCALE2)
        part = jnp.sum(weight, axis=0, keepdims=True)
        mixed = lax.dot_general(
            value, weight.astype(jnp.bfloat16), (((0,), (0,)), ((), ())), preferred_element_type=jnp.float32
        )
        total = part if total is None else total + part
        mixture = mixed if mixture is None else mixture + mixed
    return mixture * (1.0 / total), top * SCALE2 + jnp.log2(total)


def own_slab(schedule, place, k, v):
    at = columns(schedule, place)
    return k[:, at], v[:, at], schedule[WIDE + place] == 1


def tall_slabs(schedule, place, slot, heights):
    tall = schedule[TALL + place]
    if len(heights) == 2:
        heights = [piece.at[which] for piece in heights for which in range(2)]
    return [
        (heights[0][slot], heights[1][slot], tall * schedule[UP_OK] == 1),
        (heights[2][slot], heights[3][slot], tall * schedule[DOWN_OK] == 1),
    ]


def partial_kernel(schedule, q, k, v, *refs):
    heights, (out, levels) = refs[:-2], refs[-2:]
    a = q.shape[0]
    rows = levels.shape[0]
    levels[...] = jnp.zeros_like(levels)

    def body(place):
        slabs = [own_slab(schedule, place, k, v)] + tall_slabs(schedule, place, place, heights)
        mixture, level = attend(q[place], slabs)
        out[pl.ds(pl.multiple_of(place * HD, HD), HD), :] = mixture.astype(out.dtype)
        levels[pl.ds(place, 1), :] = level

    each(a, body)
    level = levels[...]
    pieces = []
    for _ in range(3):
        piece = level.astype(jnp.bfloat16)
        level = level - piece.astype(jnp.float32)
        pieces.append(piece)
    for place, piece in enumerate(pieces):
        out[pl.ds(a * HD + place * rows, rows), :] = piece


def partial_attention(schedule, q, k, v, heights):
    a = q.shape[0]
    return call(
        partial_kernel,
        schedule,
        [q, k, v, *heights],
        [jax.ShapeDtypeStruct((a * HD + 3 * levels_of(a), ROWS), jnp.bfloat16)],
        scratch=[pltpu.VMEM((levels_of(a), ROWS), jnp.float32)],
        cost=SHORT,
        name="partial_attention",
    )[0]


def local_kernel(schedule, q, k, v, *refs):
    heights, (mix, stat) = refs[:-2], refs[-2:]

    def body(place):
        slabs = [own_slab(schedule, place, k, v)] + tall_slabs(schedule, place, place, heights)
        mixture, level = attend(q[:, columns(schedule, place)], slabs)
        mix[place] = mixture
        stat[pl.ds(place, 1), :] = level

    each(mix.shape[0], body)


def local_attention(schedule, q, k, v, heights, a):
    return call(
        local_kernel,
        schedule,
        [q, k, v, *heights],
        [
            jax.ShapeDtypeStruct((a, HD, ROWS), jnp.float32),
            jax.ShapeDtypeStruct((levels_of(a), ROWS), jnp.float32),
        ],
        cost=SHORT,
        name="local_attention",
    )


def alone_kernel(first, schedule, q, k, v, out, result, sems):
    def body(slot):
        place = first + slot
        return attend(q[:, columns(schedule, place)], [own_slab(schedule, place, k, v)])[0].T

    store_columns(schedule, first, result.shape[0], out, result, sems, body)


def store_columns(schedule, first, count, out, result, sems, body):
    def one(slot):
        result[slot] = body(slot).astype(result.dtype)
        pltpu.make_async_copy(result.at[slot], out.at[:, columns(schedule, first + slot)], sems.at[slot]).start()

    def done(slot):
        pltpu.make_async_copy(result.at[slot], out.at[:, columns(schedule, first + slot)], sems.at[slot]).wait()

    each(count, one)
    each(count, done)


def side_ok(schedule, place, side):
    timed = schedule[TIMED + place]
    return (timed if side is None else timed * schedule[SIDE_OK + side]) == 1


def timed_kernel(a, sides, schedule, q, k, v, *refs):
    parts = refs[: len(sides)]
    out, result, sems = refs[-3:]

    def body(slot):
        place = a + slot
        slabs = [own_slab(schedule, place, k, v)]
        for side, part in zip(sides, parts):
            slabs.append((part[0, slot], part[1, slot], side_ok(schedule, place, side)))
        return attend(q[:, columns(schedule, place)], slabs)[0].T

    store_columns(schedule, a, result.shape[0], out, result, sems, body)


def tall_kernel(first, schedule, q, k, v, up, down, *refs):
    out, result, sems = refs[-3:]

    def body(slot):
        place = first + slot
        slabs = [own_slab(schedule, place, k, v)] + tall_slabs(schedule, place, slot, [up, down])
        return attend(q[:, columns(schedule, place)], slabs)[0].T

    store_columns(schedule, first, result.shape[0], out, result, sems, body)


def combine_kernel(sides, schedule, mix, stat, *refs):
    parts = refs[: len(sides)]
    out, result, sems, levels = refs[-4:]
    a, rows = mix.shape[0], stat.shape[0]
    for which, part in enumerate(parts):
        levels[which] = sum(part[pl.ds(a * HD + place * rows, rows), :].astype(jnp.float32) for place in range(3))

    def body(slot):
        every, mixtures = [stat[pl.ds(slot, 1), :]], [mix[slot]]
        for which, (side, part) in enumerate(zip(sides, parts)):
            level = levels[which, pl.ds(slot, 1), :]
            every.append(jnp.where(side_ok(schedule, slot, side), level, jnp.float32(MASKED)))
            mixtures.append(part[pl.ds(pl.multiple_of(slot * HD, HD), HD), :].astype(jnp.float32))
        top = functools.reduce(jnp.maximum, every)
        shares = [jnp.exp2(level - top) for level in every]
        inverse = 1.0 / functools.reduce(jnp.add, shares)
        return functools.reduce(jnp.add, [(share * inverse) * mixture for share, mixture in zip(shares, mixtures)]).T

    store_columns(schedule, 0, a, out, result, sems, body)


def into_columns(kernel, schedule, operands, out, count, scratch, cost, name):
    operands, aliases = (operands, {}) if out is None else ([*operands, out], {1 + len(operands): 0})
    return call(
        kernel,
        schedule,
        operands,
        [jax.ShapeDtypeStruct((ROWS, HEADS * HD), jnp.bfloat16)],
        scratch=[pltpu.VMEM((count, ROWS, HD), jnp.bfloat16), pltpu.SemaphoreType.DMA((count,)), *scratch],
        specs=[VMEM] * (len(operands) - len(aliases)) + [ANY] * len(aliases),
        out_specs=[ANY],
        aliases=aliases,
        cost=cost,
        name=name,
    )[0]


def after(value, *earlier):
    return lax.optimization_barrier((value, *earlier))[0]


def branch(a, b, c, time_tiles, q, k, v, schedule):
    count = time_tiles * HT
    if time_tiles == 2:
        routes = [[(i, (i + HT) % count) for i in range(count)]]
        sides = [None]
    else:
        routes = [[(i, i + HT) for i in range(count - HT)], [(i + HT, i) for i in range(count - HT)]]
        sides = [0, 1]
    backs = [[(there, here) for here, there in route] for route in routes]
    upward = [(i, i + 1) for i in range(count - 1) if i % HT != HT - 1]
    downward = [(there, here) for here, there in upward]

    def move(value, pairs):
        return lax.ppermute(value, "context", pairs)

    d = HEADS - a - b - c
    apart = a >= 2 * b and not d
    (queries,) = pack(schedule, [q], [(0, a)], True, PACK_LIMIT)
    sent = [move(queries, route) for route in routes]
    pieces = pack(schedule, after([k, v], queries), [(0, a), (a, b), (a + b, c)], apart)
    nears = [pieces.pop(0) for _ in range(2 if apart else 1)]
    across = pieces.pop(0) if b else None
    later = pieces.pop(0) if c else None
    near = [move(piece, pairs) for pairs in (upward, downward) for piece in nears]
    if b:
        across = after(across, *sent)
        others = [move(across, pairs) for pairs in routes]
    out, ready = None, schedule
    if d:
        kernel = functools.partial(alone_kernel, a + b + c)
        out = into_columns(kernel, after(schedule, *sent), [q, k, v], None, d, [], hint(FILL), "alone")
        ready = after(schedule, out)
    parts = [partial_attention(ready, query, k, v, near) for query in sent]
    if c:
        later = after(later, *(sent if out is None else [out]))
        heights = [move(later, upward), move(later, downward)]
    mix, stat = local_attention(after(schedule, *parts), q, k, v, near, a)
    parts = [move(part, back) for part, back in zip(parts, backs)]
    if b:
        kernel = functools.partial(timed_kernel, a, sides)
        out = into_columns(kernel, after(schedule, stat), [q, k, v, *others], out, b, [], hint(WAIT), "timed")
    if c:
        kernel = functools.partial(tall_kernel, a + b)
        out = into_columns(kernel, after(schedule, stat), [q, k, v, *heights], out, c, [], LONG, "tall")
    scratch = [pltpu.VMEM((len(sides), levels_of(a), ROWS), jnp.float32)]
    return into_columns(
        functools.partial(combine_kernel, sides[::-1]), schedule, [mix, stat, *parts], out, a, scratch, LONG, "combine"
    )


def local(query_rows, key_rows, value_rows, extents):
    time_tiles = lax.axis_size("context") // HT
    index = lax.axis_index("context").astype(jnp.int32).reshape(1)
    schedule, choice = plan(extents, index, time_tiles)
    branches = [functools.partial(branch, *sizes, time_tiles) for sizes in MENU]
    return lax.switch(choice.reshape(()), branches, query_rows, key_rows, value_rows, schedule)


def solution(mesh):
    placed = P(("groups", "context"), None)
    return jax.shard_map(local, mesh=mesh, in_specs=(placed, placed, placed, P()), out_specs=placed, check_vma=False)
```

```python
import functools
import math

import jax
import jax.numpy as jnp
from jax import lax
from jax.experimental import pallas as pl
from jax.experimental.pallas import tpu as pltpu
from jax.sharding import PartitionSpec as P

HEADS = 12
HD = 128
HT = 8
ROWS = 256
MASKED = -1e30
SCALE2 = math.log2(math.e) / math.sqrt(HD)
PACK_LIMIT = 62
FILL = 8e9
WAIT = 8e9
MENU = ((2, 2, 3), (3, 2, 3), (3, 2, 4), (4, 2, 3), (4, 2, 4), (5, 2, 4), (6, 2, 3), (7, 2, 2), (9, 1, 1), (12, 0, 0))

TALL, WIDE, TIMED, UP_OK, DOWN_OK, SIDE_OK = 12, 24, 36, 48, 49, 50
SCHEDULE = 64
ANY = pl.BlockSpec(memory_space=pl.ANY)
VMEM = pl.BlockSpec(memory_space=pltpu.VMEM)
SMEM = pl.BlockSpec(memory_space=pltpu.SMEM)


def plan_kernel(time_tiles, extents, index, schedule, chosen):
    one, none = jnp.int32(1), jnp.int32(0)
    wide, timed, tall = [], [], []
    for head in range(HEADS):
        wide.append(jnp.where((extents[2, head] - 1) // 2 >= 0, one, none))
        timed.append(jnp.where((extents[0, head] - 1) // 2 >= 1, one, none))
        tall.append(jnp.where((extents[1, head] - 1) // 2 >= 1, one, none))
    both = sum(t * h for t, h in zip(timed, tall))
    only_timed = sum(timed) - both
    only_tall = sum(tall) - both
    choice, a, b, c = (jnp.int32(x) for x in (len(MENU) - 1, *MENU[-1]))
    for place in reversed(range(len(MENU) - 1)):
        sizes = MENU[place]
        fits = both + jnp.maximum(only_timed - sizes[1], 0) + jnp.maximum(only_tall - sizes[2], 0) <= sizes[0]
        choice, a, b, c = (jnp.where(fits, jnp.int32(x), y) for x, y in zip((place, *sizes), (choice, a, b, c)))
    timed_in_a = jnp.maximum(only_timed - b, 0)
    tall_in_a = jnp.maximum(only_tall - c, 0)
    end_a = both + timed_in_a + tall_in_a
    end_b = a + only_timed - timed_in_a
    end_c = a + b + only_tall - tall_in_a
    seen = [none] * 4
    for head in range(HEADS):
        t, h = timed[head] == 1, tall[head] == 1
        rank = jnp.where(t, jnp.where(h, seen[0], seen[1]), jnp.where(h, seen[2], seen[3]))
        from_timed = jnp.where(rank < timed_in_a, both + rank, a + rank - timed_in_a)
        from_tall = jnp.where(rank < tall_in_a, both + timed_in_a + rank, a + b + rank - tall_in_a)
        left = rank - (a - end_a)
        later = left - (a + b - end_b)
        last = later - (a + b + c - end_c)
        free = jnp.where(
            left < 0, end_a + rank, jnp.where(later < 0, end_b + left, jnp.where(last < 0, end_c + later, a + b + c + last))
        )
        place = jnp.where(t, jnp.where(h, rank, from_timed), jnp.where(h, from_tall, free))
        for kind, is_kind in enumerate((t & h, t & ~h, ~t & h, ~t & ~h)):
            seen[kind] = seen[kind] + jnp.where(is_kind, one, none)
        schedule[place] = jnp.int32(head)
        schedule[TALL + place] = tall[head]
        schedule[WIDE + place] = wide[head]
        schedule[TIMED + place] = timed[head]
    time_index, height_index = lax.div(index[0], jnp.int32(HT)), lax.rem(index[0], jnp.int32(HT))
    schedule[UP_OK] = jnp.where(height_index > 0, one, none)
    schedule[DOWN_OK] = jnp.where(height_index < HT - 1, one, none)
    schedule[SIDE_OK] = jnp.where(time_index > 0, one, none)
    schedule[SIDE_OK + 1] = jnp.where(time_index < time_tiles - 1, one, none)
    chosen[0] = choice
    for place in range(SIDE_OK + 2, SCHEDULE):
        schedule[place] = none


def plan(extents, index, time_tiles):
    return pl.pallas_call(
        functools.partial(plan_kernel, time_tiles),
        out_shape=[jax.ShapeDtypeStruct((SCHEDULE,), jnp.int32), jax.ShapeDtypeStruct((1,), jnp.int32)],
        in_specs=[SMEM, SMEM],
        out_specs=[SMEM, SMEM],
        name="plan",
    )(extents.T, index)


def each(count, body):
    def one(place, carry):
        body(place)
        return carry

    if count > 1:
        lax.fori_loop(0, count, one, 0)
    elif count:
        body(0)


def levels_of(a):
    return -(-a // 8) * 8


def columns(schedule, place):
    return pl.ds(pl.multiple_of(schedule[place] * HD, HD), HD)


def call(kernel, schedule, operands, outs, scratch=(), specs=None, out_specs=None, aliases=None, cost=None, name=None, limit=40):
    return pl.pallas_call(
        kernel,
        out_shape=outs,
        grid_spec=pltpu.PrefetchScalarGridSpec(
            num_scalar_prefetch=1,
            in_specs=specs or [VMEM] * len(operands),
            out_specs=out_specs or [VMEM] * len(outs),
            scratch_shapes=list(scratch),
        ),
        input_output_aliases=aliases or {},
        compiler_params=pltpu.CompilerParams(vmem_limit_bytes=limit * 2**20),
        cost_estimate=cost,
        name=name,
    )(schedule, *operands)


LONG = pl.CostEstimate(flops=10**11, bytes_accessed=10**6, transcendentals=0)
SHORT = pl.CostEstimate(flops=10**6, bytes_accessed=10**5, transcendentals=0)


def hint(flops):
    return pl.CostEstimate(flops=int(flops), bytes_accessed=10**5, transcendentals=0)


def pack_kernel(firsts, sources, apart, schedule, *refs):
    inputs, outs, sems = refs[:sources], list(refs[sources:-1]), refs[-1]
    if apart:
        outs[:sources] = [outs[:sources]]

    def copies(act):
        for first, out in zip(firsts, outs):
            for which, source in enumerate(inputs):
                target = out[which] if isinstance(out, list) else out.at[which]

                def one(place):
                    at = columns(schedule, first + place)
                    act(pltpu.make_async_copy(source.at[:, at], target.at[place], sems.at[first + place, which]))

                each(target.shape[0], one)

    copies(lambda copy: copy.start())
    copies(lambda copy: copy.wait())


def pack(schedule, sources, pieces, apart, limit=40):
    pieces = [(first, size) for first, size in pieces if size]
    shapes = [(len(sources), size, ROWS, HD) for _, size in pieces]
    if apart:
        shapes[:1] = [shapes[0][1:]] * len(sources)
    return list(call(
        functools.partial(pack_kernel, [first for first, _ in pieces], len(sources), apart),
        schedule,
        sources,
        [jax.ShapeDtypeStruct(shape, sources[0].dtype) for shape in shapes],
        scratch=[pltpu.SemaphoreType.DMA((HEADS, len(sources)))],
        specs=[ANY] * len(sources),
        cost=SHORT,
        name="pack",
        limit=limit,
    ))


def attend(query, slabs):
    scores, tops = [], []
    for key, _, ok in slabs:
        score = lax.dot_general(key, query, (((1,), (1,)), ((), ())), preferred_element_type=jnp.float32)
        scores.append(score)
        tops.append(jnp.where(ok, jnp.max(score, axis=0, keepdims=True), jnp.float32(MASKED)))
    top = functools.reduce(jnp.maximum, tops)
    total, mixture = None, None
    for score, (_, value, ok) in zip(scores, slabs):
        weight = jnp.exp2((score - jnp.where(ok, top, jnp.float32(-MASKED))) * SCALE2)
        part = jnp.sum(weight, axis=0, keepdims=True)
        mixed = lax.dot_general(
            value, weight.astype(jnp.bfloat16), (((0,), (0,)), ((), ())), preferred_element_type=jnp.float32
        )
        total = part if total is None else total + part
        mixture = mixed if mixture is None else mixture + mixed
    return mixture * (1.0 / total), top * SCALE2 + jnp.log2(total)


def own_slab(schedule, place, k, v):
    at = columns(schedule, place)
    return k[:, at], v[:, at], schedule[WIDE + place] == 1


def tall_slabs(schedule, place, slot, heights):
    tall = schedule[TALL + place]
    if len(heights) == 2:
        heights = [piece.at[which] for piece in heights for which in range(2)]
    return [
        (heights[0][slot], heights[1][slot], tall * schedule[UP_OK] == 1),
        (heights[2][slot], heights[3][slot], tall * schedule[DOWN_OK] == 1),
    ]


def partial_kernel(schedule, q, k, v, *refs):
    heights, (out, levels) = refs[:-2], refs[-2:]
    a = q.shape[0]
    rows = levels.shape[0]
    levels[...] = jnp.zeros_like(levels)

    def body(place):
        slabs = [own_slab(schedule, place, k, v)] + tall_slabs(schedule, place, place, heights)
        mixture, level = attend(q[place], slabs)
        out[pl.ds(pl.multiple_of(place * HD, HD), HD), :] = mixture.astype(out.dtype)
        levels[pl.ds(place, 1), :] = level

    each(a, body)
    level = levels[...]
    pieces = []
    for _ in range(3):
        piece = level.astype(jnp.bfloat16)
        level = level - piece.astype(jnp.float32)
        pieces.append(piece)
    for place, piece in enumerate(pieces):
        out[pl.ds(a * HD + place * rows, rows), :] = piece


def partial_attention(schedule, q, k, v, heights):
    a = q.shape[0]
    return call(
        partial_kernel,
        schedule,
        [q, k, v, *heights],
        [jax.ShapeDtypeStruct((a * HD + 3 * levels_of(a), ROWS), jnp.bfloat16)],
        scratch=[pltpu.VMEM((levels_of(a), ROWS), jnp.float32)],
        cost=SHORT,
        name="partial_attention",
    )[0]


def local_kernel(schedule, q, k, v, *refs):
    heights, (mix, stat) = refs[:-2], refs[-2:]

    def body(place):
        slabs = [own_slab(schedule, place, k, v)] + tall_slabs(schedule, place, place, heights)
        mixture, level = attend(q[:, columns(schedule, place)], slabs)
        mix[place] = mixture
        stat[pl.ds(place, 1), :] = level

    each(mix.shape[0], body)


def local_attention(schedule, q, k, v, heights, a):
    return call(
        local_kernel,
        schedule,
        [q, k, v, *heights],
        [
            jax.ShapeDtypeStruct((a, HD, ROWS), jnp.float32),
            jax.ShapeDtypeStruct((levels_of(a), ROWS), jnp.float32),
        ],
        cost=SHORT,
        name="local_attention",
    )


def alone_kernel(first, schedule, q, k, v, out, result, sems):
    def body(slot):
        place = first + slot
        return attend(q[:, columns(schedule, place)], [own_slab(schedule, place, k, v)])[0].T

    store_columns(schedule, first, result.shape[0], out, result, sems, body)


def store_columns(schedule, first, count, out, result, sems, body):
    def one(slot):
        result[slot] = body(slot).astype(result.dtype)
        pltpu.make_async_copy(result.at[slot], out.at[:, columns(schedule, first + slot)], sems.at[slot]).start()

    def done(slot):
        pltpu.make_async_copy(result.at[slot], out.at[:, columns(schedule, first + slot)], sems.at[slot]).wait()

    each(count, one)
    each(count, done)


def side_ok(schedule, place, side):
    timed = schedule[TIMED + place]
    return (timed if side is None else timed * schedule[SIDE_OK + side]) == 1


def timed_kernel(a, sides, schedule, q, k, v, *refs):
    parts = refs[: len(sides)]
    out, result, sems = refs[-3:]

    def body(slot):
        place = a + slot
        slabs = [own_slab(schedule, place, k, v)]
        for side, part in zip(sides, parts):
            slabs.append((part[0, slot], part[1, slot], side_ok(schedule, place, side)))
        return attend(q[:, columns(schedule, place)], slabs)[0].T

    store_columns(schedule, a, result.shape[0], out, result, sems, body)


def tall_kernel(first, schedule, q, k, v, up, down, *refs):
    out, result, sems = refs[-3:]

    def body(slot):
        place = first + slot
        slabs = [own_slab(schedule, place, k, v)] + tall_slabs(schedule, place, slot, [up, down])
        return attend(q[:, columns(schedule, place)], slabs)[0].T

    store_columns(schedule, first, result.shape[0], out, result, sems, body)


def combine_kernel(sides, schedule, mix, stat, *refs):
    parts = refs[: len(sides)]
    out, result, sems, levels = refs[-4:]
    a, rows = mix.shape[0], stat.shape[0]
    for which, part in enumerate(parts):
        levels[which] = sum(part[pl.ds(a * HD + place * rows, rows), :].astype(jnp.float32) for place in range(3))

    def body(slot):
        every, mixtures = [stat[pl.ds(slot, 1), :]], [mix[slot]]
        for which, (side, part) in enumerate(zip(sides, parts)):
            level = levels[which, pl.ds(slot, 1), :]
            every.append(jnp.where(side_ok(schedule, slot, side), level, jnp.float32(MASKED)))
            mixtures.append(part[pl.ds(pl.multiple_of(slot * HD, HD), HD), :].astype(jnp.float32))
        top = functools.reduce(jnp.maximum, every)
        shares = [jnp.exp2(level - top) for level in every]
        inverse = 1.0 / functools.reduce(jnp.add, shares)
        return functools.reduce(jnp.add, [(share * inverse) * mixture for share, mixture in zip(shares, mixtures)]).T

    store_columns(schedule, 0, a, out, result, sems, body)


def into_columns(kernel, schedule, operands, out, count, scratch, cost, name):
    operands, aliases = (operands, {}) if out is None else ([*operands, out], {1 + len(operands): 0})
    return call(
        kernel,
        schedule,
        operands,
        [jax.ShapeDtypeStruct((ROWS, HEADS * HD), jnp.bfloat16)],
        scratch=[pltpu.VMEM((count, ROWS, HD), jnp.bfloat16), pltpu.SemaphoreType.DMA((count,)), *scratch],
        specs=[VMEM] * (len(operands) - len(aliases)) + [ANY] * len(aliases),
        out_specs=[ANY],
        aliases=aliases,
        cost=cost,
        name=name,
    )[0]


def after(value, *earlier):
    return lax.optimization_barrier((value, *earlier))[0]


def branch(a, b, c, time_tiles, q, k, v, schedule):
    count = time_tiles * HT
    if time_tiles == 2:
        routes = [[(i, (i + HT) % count) for i in range(count)]]
        sides = [None]
    else:
        routes = [[(i, i + HT) for i in range(count - HT)], [(i + HT, i) for i in range(count - HT)]]
        sides = [0, 1]
    backs = [[(there, here) for here, there in route] for route in routes]
    upward = [(i, i + 1) for i in range(count - 1) if i % HT != HT - 1]
    downward = [(there, here) for here, there in upward]

    def move(value, pairs):
        return lax.ppermute(value, "context", pairs)

    d = HEADS - a - b - c
    apart = a >= 2 * b and not d
    (queries,) = pack(schedule, [q], [(0, a)], True, PACK_LIMIT)
    sent = [move(queries, route) for route in routes]
    pieces = pack(schedule, after([k, v], queries), [(0, a), (a, b), (a + b, c)], apart)
    nears = [pieces.pop(0) for _ in range(2 if apart else 1)]
    across = pieces.pop(0) if b else None
    later = pieces.pop(0) if c else None
    near = [move(piece, pairs) for pairs in (upward, downward) for piece in nears]
    if b:
        across = after(across, *sent)
        others = [move(across, pairs) for pairs in routes]
    out, ready = None, schedule
    if d:
        kernel = functools.partial(alone_kernel, a + b + c)
        out = into_columns(kernel, after(schedule, *sent), [q, k, v], None, d, [], hint(FILL), "alone")
        ready = after(schedule, out)
    parts = [partial_attention(ready, query, k, v, near) for query in sent]
    if c:
        later = after(later, *(sent if out is None else [out]))
        heights = [move(later, upward), move(later, downward)]
    mix, stat = local_attention(after(schedule, *parts), q, k, v, near, a)
    parts = [move(part, back) for part, back in zip(parts, backs)]
    if b:
        kernel = functools.partial(timed_kernel, a, sides)
        out = into_columns(kernel, after(schedule, stat), [q, k, v, *others], out, b, [], hint(WAIT), "timed")
    if c:
        kernel = functools.partial(tall_kernel, a + b)
        out = into_columns(kernel, after(schedule, stat), [q, k, v, *heights], out, c, [], LONG, "tall")
    scratch = [pltpu.VMEM((len(sides), levels_of(a), ROWS), jnp.float32)]
    return into_columns(
        functools.partial(combine_kernel, sides[::-1]), schedule, [mix, stat, *parts], out, a, scratch, LONG, "combine"
    )


def local(query_rows, key_rows, value_rows, extents):
    time_tiles = lax.axis_size("context") // HT
    index = lax.axis_index("context").astype(jnp.int32).reshape(1)
    schedule, choice = plan(extents, index, time_tiles)
    branches = [functools.partial(branch, *sizes, time_tiles) for sizes in MENU]
    return lax.switch(choice.reshape(()), branches, query_rows, key_rows, value_rows, schedule)


def solution(mesh):
    placed = P(("groups", "context"), None)
    return jax.shard_map(local, mesh=mesh, in_specs=(placed, placed, placed, P()), out_specs=placed, check_vma=False)
```

```python
import functools
import math

import jax
import jax.numpy as jnp
from jax import lax
from jax.experimental import pallas as pl
from jax.experimental.pallas import tpu as pltpu
from jax.sharding import PartitionSpec as P

HEADS = 12
HD = 128
HT = 8
ROWS = 256
MASKED = -1e30
SCALE2 = math.log2(math.e) / math.sqrt(HD)
PACK_LIMIT = 62
FILL_EARLY, FILL, WAIT = 2e10, 8e9, 8e9
MENU = ((2, 2, 3), (3, 2, 3), (3, 2, 4), (4, 2, 3), (4, 2, 4), (5, 2, 4), (6, 2, 3), (7, 2, 2), (9, 1, 1), (12, 0, 0))

TALL, WIDE, TIMED, UP_OK, DOWN_OK, SIDE_OK = 12, 24, 36, 48, 49, 50
SCHEDULE = 64
ANY = pl.BlockSpec(memory_space=pl.ANY)
VMEM = pl.BlockSpec(memory_space=pltpu.VMEM)
SMEM = pl.BlockSpec(memory_space=pltpu.SMEM)


def plan_kernel(time_tiles, extents, index, schedule, chosen):
    one, none = jnp.int32(1), jnp.int32(0)
    wide, timed, tall = [], [], []
    for head in range(HEADS):
        wide.append(jnp.where((extents[2, head] - 1) // 2 >= 0, one, none))
        timed.append(jnp.where((extents[0, head] - 1) // 2 >= 1, one, none))
        tall.append(jnp.where((extents[1, head] - 1) // 2 >= 1, one, none))
    both = sum(t * h for t, h in zip(timed, tall))
    only_timed = sum(timed) - both
    only_tall = sum(tall) - both
    choice, a, b, c = (jnp.int32(x) for x in (len(MENU) - 1, *MENU[-1]))
    for place in reversed(range(len(MENU) - 1)):
        sizes = MENU[place]
        fits = both + jnp.maximum(only_timed - sizes[1], 0) + jnp.maximum(only_tall - sizes[2], 0) <= sizes[0]
        choice, a, b, c = (jnp.where(fits, jnp.int32(x), y) for x, y in zip((place, *sizes), (choice, a, b, c)))
    timed_in_a = jnp.maximum(only_timed - b, 0)
    tall_in_a = jnp.maximum(only_tall - c, 0)
    end_a = both + timed_in_a + tall_in_a
    end_b = a + only_timed - timed_in_a
    end_c = a + b + only_tall - tall_in_a
    seen = [none] * 4
    for head in range(HEADS):
        t, h = timed[head] == 1, tall[head] == 1
        rank = jnp.where(t, jnp.where(h, seen[0], seen[1]), jnp.where(h, seen[2], seen[3]))
        from_timed = jnp.where(rank < timed_in_a, both + rank, a + rank - timed_in_a)
        from_tall = jnp.where(rank < tall_in_a, both + timed_in_a + rank, a + b + rank - tall_in_a)
        left = rank - (a - end_a)
        later = left - (a + b - end_b)
        last = later - (a + b + c - end_c)
        free = jnp.where(
            left < 0, end_a + rank, jnp.where(later < 0, end_b + left, jnp.where(last < 0, end_c + later, a + b + c + last))
        )
        place = jnp.where(t, jnp.where(h, rank, from_timed), jnp.where(h, from_tall, free))
        for kind, is_kind in enumerate((t & h, t & ~h, ~t & h, ~t & ~h)):
            seen[kind] = seen[kind] + jnp.where(is_kind, one, none)
        schedule[place] = jnp.int32(head)
        schedule[TALL + place] = tall[head]
        schedule[WIDE + place] = wide[head]
        schedule[TIMED + place] = timed[head]
    time_index, height_index = lax.div(index[0], jnp.int32(HT)), lax.rem(index[0], jnp.int32(HT))
    schedule[UP_OK] = jnp.where(height_index > 0, one, none)
    schedule[DOWN_OK] = jnp.where(height_index < HT - 1, one, none)
    schedule[SIDE_OK] = jnp.where(time_index > 0, one, none)
    schedule[SIDE_OK + 1] = jnp.where(time_index < time_tiles - 1, one, none)
    chosen[0] = choice
    for place in range(SIDE_OK + 2, SCHEDULE):
        schedule[place] = none


def plan(extents, index, time_tiles):
    return pl.pallas_call(
        functools.partial(plan_kernel, time_tiles),
        out_shape=[jax.ShapeDtypeStruct((SCHEDULE,), jnp.int32), jax.ShapeDtypeStruct((1,), jnp.int32)],
        in_specs=[SMEM, SMEM],
        out_specs=[SMEM, SMEM],
        name="plan",
    )(extents.T, index)


def each(count, body):
    def one(place, carry):
        body(place)
        return carry

    if count > 1:
        lax.fori_loop(0, count, one, 0)
    elif count:
        body(0)


def levels_of(a):
    return -(-a // 8) * 8


def columns(schedule, place):
    return pl.ds(pl.multiple_of(schedule[place] * HD, HD), HD)


def call(kernel, schedule, operands, outs, scratch=(), specs=None, out_specs=None, aliases=None, cost=None, name=None, limit=40):
    return pl.pallas_call(
        kernel,
        out_shape=outs,
        grid_spec=pltpu.PrefetchScalarGridSpec(
            num_scalar_prefetch=1,
            in_specs=specs or [VMEM] * len(operands),
            out_specs=out_specs or [VMEM] * len(outs),
            scratch_shapes=list(scratch),
        ),
        input_output_aliases=aliases or {},
        compiler_params=pltpu.CompilerParams(vmem_limit_bytes=limit * 2**20),
        cost_estimate=cost,
        name=name,
    )(schedule, *operands)


LONG = pl.CostEstimate(flops=10**11, bytes_accessed=10**6, transcendentals=0)
SHORT = pl.CostEstimate(flops=10**6, bytes_accessed=10**5, transcendentals=0)


def hint(flops):
    return pl.CostEstimate(flops=int(flops), bytes_accessed=10**5, transcendentals=0)


def pack_kernel(firsts, sources, apart, schedule, *refs):
    inputs, outs, sems = refs[:sources], list(refs[sources:-1]), refs[-1]
    if apart:
        outs[:sources] = [outs[:sources]]

    def copies(act):
        for first, out in zip(firsts, outs):
            for which, source in enumerate(inputs):
                target = out[which] if isinstance(out, list) else out.at[which]

                def one(place):
                    at = columns(schedule, first + place)
                    act(pltpu.make_async_copy(source.at[:, at], target.at[place], sems.at[first + place, which]))

                each(target.shape[0], one)

    copies(lambda copy: copy.start())
    copies(lambda copy: copy.wait())


def pack(schedule, sources, pieces, apart, limit=40):
    pieces = [(first, size) for first, size in pieces if size]
    shapes = [(len(sources), size, ROWS, HD) for _, size in pieces]
    if apart:
        shapes[:1] = [shapes[0][1:]] * len(sources)
    return list(call(
        functools.partial(pack_kernel, [first for first, _ in pieces], len(sources), apart),
        schedule,
        sources,
        [jax.ShapeDtypeStruct(shape, sources[0].dtype) for shape in shapes],
        scratch=[pltpu.SemaphoreType.DMA((HEADS, len(sources)))],
        specs=[ANY] * len(sources),
        cost=SHORT,
        name="pack",
        limit=limit,
    ))


def attend(query, slabs):
    scores, tops = [], []
    for key, _, ok in slabs:
        score = lax.dot_general(key, query, (((1,), (1,)), ((), ())), preferred_element_type=jnp.float32)
        scores.append(score)
        tops.append(jnp.where(ok, jnp.max(score, axis=0, keepdims=True), jnp.float32(MASKED)))
    top = functools.reduce(jnp.maximum, tops)
    total, mixture = None, None
    for score, (_, value, ok) in zip(scores, slabs):
        weight = jnp.exp2((score - jnp.where(ok, top, jnp.float32(-MASKED))) * SCALE2)
        part = jnp.sum(weight, axis=0, keepdims=True)
        mixed = lax.dot_general(
            value, weight.astype(jnp.bfloat16), (((0,), (0,)), ((), ())), preferred_element_type=jnp.float32
        )
        total = part if total is None else total + part
        mixture = mixed if mixture is None else mixture + mixed
    return mixture * (1.0 / total), top * SCALE2 + jnp.log2(total)


def own_slab(schedule, place, k, v):
    at = columns(schedule, place)
    return k[:, at], v[:, at], schedule[WIDE + place] == 1


def tall_slabs(schedule, place, slot, heights):
    tall = schedule[TALL + place]
    if len(heights) == 2:
        heights = [piece.at[which] for piece in heights for which in range(2)]
    return [
        (heights[0][slot], heights[1][slot], tall * schedule[UP_OK] == 1),
        (heights[2][slot], heights[3][slot], tall * schedule[DOWN_OK] == 1),
    ]


def partial_kernel(schedule, q, k, v, *refs):
    heights, (out, levels) = refs[:-2], refs[-2:]
    a = q.shape[0]
    rows = levels.shape[0]
    levels[...] = jnp.zeros_like(levels)

    def body(place):
        slabs = [own_slab(schedule, place, k, v)] + tall_slabs(schedule, place, place, heights)
        mixture, level = attend(q[place], slabs)
        out[pl.ds(pl.multiple_of(place * HD, HD), HD), :] = mixture.astype(out.dtype)
        levels[pl.ds(place, 1), :] = level

    each(a, body)
    level = levels[...]
    pieces = []
    for _ in range(3):
        piece = level.astype(jnp.bfloat16)
        level = level - piece.astype(jnp.float32)
        pieces.append(piece)
    for place, piece in enumerate(pieces):
        out[pl.ds(a * HD + place * rows, rows), :] = piece


def partial_attention(schedule, q, k, v, heights):
    a = q.shape[0]
    return call(
        partial_kernel,
        schedule,
        [q, k, v, *heights],
        [jax.ShapeDtypeStruct((a * HD + 3 * levels_of(a), ROWS), jnp.bfloat16)],
        scratch=[pltpu.VMEM((levels_of(a), ROWS), jnp.float32)],
        cost=SHORT,
        name="partial_attention",
    )[0]


def local_kernel(schedule, q, k, v, *refs):
    heights, (mix, stat) = refs[:-2], refs[-2:]

    def body(place):
        slabs = [own_slab(schedule, place, k, v)] + tall_slabs(schedule, place, place, heights)
        mixture, level = attend(q[:, columns(schedule, place)], slabs)
        mix[place] = mixture
        stat[pl.ds(place, 1), :] = level

    each(mix.shape[0], body)


def local_attention(schedule, q, k, v, heights, a):
    return call(
        local_kernel,
        schedule,
        [q, k, v, *heights],
        [
            jax.ShapeDtypeStruct((a, HD, ROWS), jnp.float32),
            jax.ShapeDtypeStruct((levels_of(a), ROWS), jnp.float32),
        ],
        cost=SHORT,
        name="local_attention",
    )


def alone_kernel(first, schedule, q, k, v, out, result, sems):
    def body(slot):
        place = first + slot
        return attend(q[:, columns(schedule, place)], [own_slab(schedule, place, k, v)])[0].T

    store_columns(schedule, first, result.shape[0], out, result, sems, body)


def store_columns(schedule, first, count, out, result, sems, body):
    def one(slot):
        result[slot] = body(slot).astype(result.dtype)
        pltpu.make_async_copy(result.at[slot], out.at[:, columns(schedule, first + slot)], sems.at[slot]).start()

    def done(slot):
        pltpu.make_async_copy(result.at[slot], out.at[:, columns(schedule, first + slot)], sems.at[slot]).wait()

    each(count, one)
    each(count, done)


def side_ok(schedule, place, side):
    timed = schedule[TIMED + place]
    return (timed if side is None else timed * schedule[SIDE_OK + side]) == 1


def timed_kernel(a, sides, schedule, q, k, v, *refs):
    parts = refs[: len(sides)]
    out, result, sems = refs[-3:]

    def body(slot):
        place = a + slot
        slabs = [own_slab(schedule, place, k, v)]
        for side, part in zip(sides, parts):
            slabs.append((part[0, slot], part[1, slot], side_ok(schedule, place, side)))
        return attend(q[:, columns(schedule, place)], slabs)[0].T

    store_columns(schedule, a, result.shape[0], out, result, sems, body)


def tall_kernel(first, schedule, q, k, v, up, down, *refs):
    out, result, sems = refs[-3:]

    def body(slot):
        place = first + slot
        slabs = [own_slab(schedule, place, k, v)] + tall_slabs(schedule, place, slot, [up, down])
        return attend(q[:, columns(schedule, place)], slabs)[0].T

    store_columns(schedule, first, result.shape[0], out, result, sems, body)


def combine_kernel(sides, schedule, mix, stat, *refs):
    parts = refs[: len(sides)]
    out, result, sems, levels = refs[-4:]
    a, rows = mix.shape[0], stat.shape[0]
    for which, part in enumerate(parts):
        levels[which] = sum(part[pl.ds(a * HD + place * rows, rows), :].astype(jnp.float32) for place in range(3))

    def body(slot):
        every, mixtures = [stat[pl.ds(slot, 1), :]], [mix[slot]]
        for which, (side, part) in enumerate(zip(sides, parts)):
            level = levels[which, pl.ds(slot, 1), :]
            every.append(jnp.where(side_ok(schedule, slot, side), level, jnp.float32(MASKED)))
            mixtures.append(part[pl.ds(pl.multiple_of(slot * HD, HD), HD), :].astype(jnp.float32))
        top = functools.reduce(jnp.maximum, every)
        shares = [jnp.exp2(level - top) for level in every]
        inverse = 1.0 / functools.reduce(jnp.add, shares)
        return functools.reduce(jnp.add, [(share * inverse) * mixture for share, mixture in zip(shares, mixtures)]).T

    store_columns(schedule, 0, a, out, result, sems, body)


def into_columns(kernel, schedule, operands, out, count, scratch, cost, name):
    operands, aliases = (operands, {}) if out is None else ([*operands, out], {1 + len(operands): 0})
    return call(
        kernel,
        schedule,
        operands,
        [jax.ShapeDtypeStruct((ROWS, HEADS * HD), jnp.bfloat16)],
        scratch=[pltpu.VMEM((count, ROWS, HD), jnp.bfloat16), pltpu.SemaphoreType.DMA((count,)), *scratch],
        specs=[VMEM] * (len(operands) - len(aliases)) + [ANY] * len(aliases),
        out_specs=[ANY],
        aliases=aliases,
        cost=cost,
        name=name,
    )[0]


def after(value, *earlier):
    return lax.optimization_barrier((value, *earlier))[0]


def branch(a, b, c, time_tiles, q, k, v, schedule):
    count = time_tiles * HT
    if time_tiles == 2:
        routes = [[(i, (i + HT) % count) for i in range(count)]]
        sides = [None]
    else:
        routes = [[(i, i + HT) for i in range(count - HT)], [(i + HT, i) for i in range(count - HT)]]
        sides = [0, 1]
    backs = [[(there, here) for here, there in route] for route in routes]
    upward = [(i, i + 1) for i in range(count - 1) if i % HT != HT - 1]
    downward = [(there, here) for here, there in upward]

    def move(value, pairs):
        return lax.ppermute(value, "context", pairs)

    d = HEADS - a - b - c
    apart = a >= 2 * b and not d
    (queries,) = pack(schedule, [q], [(0, a)], True, PACK_LIMIT)
    sent = [move(queries, route) for route in routes]
    pieces = pack(schedule, after([k, v], queries), [(0, a), (a, b), (a + b, c)], apart)
    nears = [pieces.pop(0) for _ in range(2 if apart else 1)]
    across = pieces.pop(0) if b else None
    later = pieces.pop(0) if c else None
    near = [move(piece, pairs) for pairs in (upward, downward) for piece in nears]
    early = a == 4
    out, ready = None, schedule
    if d:
        kernel = functools.partial(alone_kernel, a + b + c)
        first = after(schedule, *(nears if early else sent))
        out = into_columns(kernel, first, [q, k, v], None, d, [], hint(FILL_EARLY if early else FILL), "alone")
        ready = schedule if early else after(schedule, out)
    if b:
        across = after(across, *([out] if d and early else sent))
        others = [move(across, pairs) for pairs in routes]
    parts = [partial_attention(ready, query, k, v, near) for query in sent]
    if c:
        later = after(later, *([out] if d else sent))
        heights = [move(later, upward), move(later, downward)]
    mix, stat = local_attention(after(schedule, *parts), q, k, v, near, a)
    parts = [move(part, back) for part, back in zip(parts, backs)]
    if b:
        kernel = functools.partial(timed_kernel, a, sides)
        out = into_columns(kernel, after(schedule, stat), [q, k, v, *others], out, b, [], hint(WAIT), "timed")
    if c:
        kernel = functools.partial(tall_kernel, a + b)
        out = into_columns(kernel, after(schedule, stat), [q, k, v, *heights], out, c, [], LONG, "tall")
    scratch = [pltpu.VMEM((len(sides), levels_of(a), ROWS), jnp.float32)]
    return into_columns(
        functools.partial(combine_kernel, sides[::-1]), schedule, [mix, stat, *parts], out, a, scratch, LONG, "combine"
    )


def local(query_rows, key_rows, value_rows, extents):
    time_tiles = lax.axis_size("context") // HT
    index = lax.axis_index("context").astype(jnp.int32).reshape(1)
    schedule, choice = plan(extents, index, time_tiles)
    branches = [functools.partial(branch, *sizes, time_tiles) for sizes in MENU]
    return lax.switch(choice.reshape(()), branches, query_rows, key_rows, value_rows, schedule)


def solution(mesh):
    placed = P(("groups", "context"), None)
    return jax.shard_map(local, mesh=mesh, in_specs=(placed, placed, placed, P()), out_specs=placed, check_vma=False)
```

```python
import functools
import math

import jax
import jax.numpy as jnp
from jax import lax
from jax.experimental import pallas as pl
from jax.experimental.pallas import tpu as pltpu
from jax.sharding import PartitionSpec as P

HEADS = 12
HD = 128
HT = 8
ROWS = 256
MASKED = -1e30
SCALE2 = math.log2(math.e) / math.sqrt(HD)
PACK_LIMIT = 62
FILL_EARLY, FILL, WAIT = 2e10, 8e9, 8e9
MENU = ((2, 2, 3), (3, 2, 3), (3, 2, 4), (4, 2, 3), (4, 2, 4), (5, 2, 4), (6, 2, 3), (7, 2, 2), (9, 1, 1), (12, 0, 0))

TALL, WIDE, TIMED, UP_OK, DOWN_OK, SIDE_OK = 12, 24, 36, 48, 49, 50
SCHEDULE = 64
ANY = pl.BlockSpec(memory_space=pl.ANY)
VMEM = pl.BlockSpec(memory_space=pltpu.VMEM)
SMEM = pl.BlockSpec(memory_space=pltpu.SMEM)


def plan_kernel(time_tiles, extents, index, schedule, chosen):
    one, none = jnp.int32(1), jnp.int32(0)
    wide, timed, tall = [], [], []
    for head in range(HEADS):
        wide.append(jnp.where((extents[2, head] - 1) // 2 >= 0, one, none))
        timed.append(jnp.where((extents[0, head] - 1) // 2 >= 1, one, none))
        tall.append(jnp.where((extents[1, head] - 1) // 2 >= 1, one, none))
    both = sum(t * h for t, h in zip(timed, tall))
    only_timed = sum(timed) - both
    only_tall = sum(tall) - both
    choice, a, b, c = (jnp.int32(x) for x in (len(MENU) - 1, *MENU[-1]))
    for place in reversed(range(len(MENU) - 1)):
        sizes = MENU[place]
        fits = both + jnp.maximum(only_timed - sizes[1], 0) + jnp.maximum(only_tall - sizes[2], 0) <= sizes[0]
        choice, a, b, c = (jnp.where(fits, jnp.int32(x), y) for x, y in zip((place, *sizes), (choice, a, b, c)))
    timed_in_a = jnp.maximum(only_timed - b, 0)
    tall_in_a = jnp.maximum(only_tall - c, 0)
    end_a = both + timed_in_a + tall_in_a
    end_b = a + only_timed - timed_in_a
    end_c = a + b + only_tall - tall_in_a
    seen = [none] * 4
    for head in range(HEADS):
        t, h = timed[head] == 1, tall[head] == 1
        rank = jnp.where(t, jnp.where(h, seen[0], seen[1]), jnp.where(h, seen[2], seen[3]))
        from_timed = jnp.where(rank < timed_in_a, both + rank, a + rank - timed_in_a)
        from_tall = jnp.where(rank < tall_in_a, both + timed_in_a + rank, a + b + rank - tall_in_a)
        left = rank - (a - end_a)
        later = left - (a + b - end_b)
        last = later - (a + b + c - end_c)
        free = jnp.where(
            left < 0, end_a + rank, jnp.where(later < 0, end_b + left, jnp.where(last < 0, end_c + later, a + b + c + last))
        )
        place = jnp.where(t, jnp.where(h, rank, from_timed), jnp.where(h, from_tall, free))
        for kind, is_kind in enumerate((t & h, t & ~h, ~t & h, ~t & ~h)):
            seen[kind] = seen[kind] + jnp.where(is_kind, one, none)
        schedule[place] = jnp.int32(head)
        schedule[TALL + place] = tall[head]
        schedule[WIDE + place] = wide[head]
        schedule[TIMED + place] = timed[head]
    time_index, height_index = lax.div(index[0], jnp.int32(HT)), lax.rem(index[0], jnp.int32(HT))
    schedule[UP_OK] = jnp.where(height_index > 0, one, none)
    schedule[DOWN_OK] = jnp.where(height_index < HT - 1, one, none)
    schedule[SIDE_OK] = jnp.where(time_index > 0, one, none)
    schedule[SIDE_OK + 1] = jnp.where(time_index < time_tiles - 1, one, none)
    chosen[0] = choice
    for place in range(SIDE_OK + 2, SCHEDULE):
        schedule[place] = none


def plan(extents, index, time_tiles):
    return pl.pallas_call(
        functools.partial(plan_kernel, time_tiles),
        out_shape=[jax.ShapeDtypeStruct((SCHEDULE,), jnp.int32), jax.ShapeDtypeStruct((1,), jnp.int32)],
        in_specs=[SMEM, SMEM],
        out_specs=[SMEM, SMEM],
        name="plan",
    )(extents.T, index)


def each(count, body):
    def one(place, carry):
        body(place)
        return carry

    if count > 1:
        lax.fori_loop(0, count, one, 0)
    elif count:
        body(0)


def levels_of(a):
    return -(-a // 8) * 8


def columns(schedule, place):
    return pl.ds(pl.multiple_of(schedule[place] * HD, HD), HD)


def call(kernel, schedule, operands, outs, scratch=(), specs=None, out_specs=None, aliases=None, cost=None, name=None, limit=40):
    return pl.pallas_call(
        kernel,
        out_shape=outs,
        grid_spec=pltpu.PrefetchScalarGridSpec(
            num_scalar_prefetch=1,
            in_specs=specs or [VMEM] * len(operands),
            out_specs=out_specs or [VMEM] * len(outs),
            scratch_shapes=list(scratch),
        ),
        input_output_aliases=aliases or {},
        compiler_params=pltpu.CompilerParams(vmem_limit_bytes=limit * 2**20),
        cost_estimate=cost,
        name=name,
    )(schedule, *operands)


LONG = pl.CostEstimate(flops=10**11, bytes_accessed=10**6, transcendentals=0)
SHORT = pl.CostEstimate(flops=10**6, bytes_accessed=10**5, transcendentals=0)


def hint(flops):
    return pl.CostEstimate(flops=int(flops), bytes_accessed=10**5, transcendentals=0)


def pack_kernel(firsts, sources, apart, schedule, *refs):
    inputs, outs, sems = refs[:sources], list(refs[sources:-1]), refs[-1]
    if apart:
        outs[:sources] = [outs[:sources]]

    def copies(act):
        for first, out in zip(firsts, outs):
            for which, source in enumerate(inputs):
                target = out[which] if isinstance(out, list) else out.at[which]

                def one(place):
                    at = columns(schedule, first + place)
                    act(pltpu.make_async_copy(source.at[:, at], target.at[place], sems.at[first + place, which]))

                each(target.shape[0], one)

    copies(lambda copy: copy.start())
    copies(lambda copy: copy.wait())


def pack(schedule, sources, pieces, apart, limit=40):
    pieces = [(first, size) for first, size in pieces if size]
    shapes = [(len(sources), size, ROWS, HD) for _, size in pieces]
    if apart:
        shapes[:1] = [shapes[0][1:]] * len(sources)
    return list(call(
        functools.partial(pack_kernel, [first for first, _ in pieces], len(sources), apart),
        schedule,
        sources,
        [jax.ShapeDtypeStruct(shape, sources[0].dtype) for shape in shapes],
        scratch=[pltpu.SemaphoreType.DMA((HEADS, len(sources)))],
        specs=[ANY] * len(sources),
        cost=SHORT,
        name="pack",
        limit=limit,
    ))


def attend(query, slabs):
    scores, tops = [], []
    for key, _, ok in slabs:
        score = lax.dot_general(key, query, (((1,), (1,)), ((), ())), preferred_element_type=jnp.float32)
        scores.append(score)
        tops.append(jnp.where(ok, jnp.max(score, axis=0, keepdims=True), jnp.float32(MASKED)))
    top = functools.reduce(jnp.maximum, tops)
    total, mixture = None, None
    for score, (_, value, ok) in zip(scores, slabs):
        weight = jnp.exp2((score - jnp.where(ok, top, jnp.float32(-MASKED))) * SCALE2)
        part = jnp.sum(weight, axis=0, keepdims=True)
        mixed = lax.dot_general(
            value, weight.astype(jnp.bfloat16), (((0,), (0,)), ((), ())), preferred_element_type=jnp.float32
        )
        total = part if total is None else total + part
        mixture = mixed if mixture is None else mixture + mixed
    return mixture * (1.0 / total), top * SCALE2 + jnp.log2(total)


def own_slab(schedule, place, k, v):
    at = columns(schedule, place)
    return k[:, at], v[:, at], schedule[WIDE + place] == 1


def tall_slabs(schedule, place, slot, heights):
    tall = schedule[TALL + place]
    if len(heights) == 2:
        heights = [piece.at[which] for piece in heights for which in range(2)]
    return [
        (heights[0][slot], heights[1][slot], tall * schedule[UP_OK] == 1),
        (heights[2][slot], heights[3][slot], tall * schedule[DOWN_OK] == 1),
    ]


def partial_kernel(schedule, q, k, v, *refs):
    heights, (out, levels) = refs[:-2], refs[-2:]
    a = q.shape[0]
    rows = levels.shape[0]
    levels[...] = jnp.zeros_like(levels)

    def body(place):
        slabs = [own_slab(schedule, place, k, v)] + tall_slabs(schedule, place, place, heights)
        mixture, level = attend(q[place], slabs)
        out[pl.ds(pl.multiple_of(place * HD, HD), HD), :] = mixture.astype(out.dtype)
        levels[pl.ds(place, 1), :] = level

    each(a, body)
    level = levels[...]
    pieces = []
    for _ in range(3):
        piece = level.astype(jnp.bfloat16)
        level = level - piece.astype(jnp.float32)
        pieces.append(piece)
    for place, piece in enumerate(pieces):
        out[pl.ds(a * HD + place * rows, rows), :] = piece


def partial_attention(schedule, q, k, v, heights):
    a = q.shape[0]
    return call(
        partial_kernel,
        schedule,
        [q, k, v, *heights],
        [jax.ShapeDtypeStruct((a * HD + 3 * levels_of(a), ROWS), jnp.bfloat16)],
        scratch=[pltpu.VMEM((levels_of(a), ROWS), jnp.float32)],
        cost=SHORT,
        name="partial_attention",
    )[0]


def local_kernel(schedule, q, k, v, *refs):
    heights, (mix, stat) = refs[:-2], refs[-2:]

    def body(place):
        slabs = [own_slab(schedule, place, k, v)] + tall_slabs(schedule, place, place, heights)
        mixture, level = attend(q[:, columns(schedule, place)], slabs)
        mix[place] = mixture
        stat[pl.ds(place, 1), :] = level

    each(mix.shape[0], body)


def local_attention(schedule, q, k, v, heights, a):
    return call(
        local_kernel,
        schedule,
        [q, k, v, *heights],
        [
            jax.ShapeDtypeStruct((a, HD, ROWS), jnp.float32),
            jax.ShapeDtypeStruct((levels_of(a), ROWS), jnp.float32),
        ],
        cost=SHORT,
        name="local_attention",
    )


def alone_kernel(first, schedule, q, k, v, out, result, sems):
    def body(slot):
        place = first + slot
        return attend(q[:, columns(schedule, place)], [own_slab(schedule, place, k, v)])[0].T

    store_columns(schedule, first, result.shape[0], out, result, sems, body)


def store_columns(schedule, first, count, out, result, sems, body):
    def one(slot):
        result[slot] = body(slot).astype(result.dtype)
        pltpu.make_async_copy(result.at[slot], out.at[:, columns(schedule, first + slot)], sems.at[slot]).start()

    def done(slot):
        pltpu.make_async_copy(result.at[slot], out.at[:, columns(schedule, first + slot)], sems.at[slot]).wait()

    each(count, one)
    each(count, done)


def side_ok(schedule, place, side):
    timed = schedule[TIMED + place]
    return (timed if side is None else timed * schedule[SIDE_OK + side]) == 1


def timed_kernel(a, sides, schedule, q, k, v, *refs):
    parts = refs[: len(sides)]
    out, result, sems = refs[-3:]

    def body(slot):
        place = a + slot
        slabs = [own_slab(schedule, place, k, v)]
        for side, part in zip(sides, parts):
            slabs.append((part[0, slot], part[1, slot], side_ok(schedule, place, side)))
        return attend(q[:, columns(schedule, place)], slabs)[0].T

    store_columns(schedule, a, result.shape[0], out, result, sems, body)


def tall_kernel(first, schedule, q, k, v, up, down, *refs):
    out, result, sems = refs[-3:]

    def body(slot):
        place = first + slot
        slabs = [own_slab(schedule, place, k, v)] + tall_slabs(schedule, place, slot, [up, down])
        return attend(q[:, columns(schedule, place)], slabs)[0].T

    store_columns(schedule, first, result.shape[0], out, result, sems, body)


def combine_kernel(sides, schedule, mix, stat, *refs):
    parts = refs[: len(sides)]
    out, result, sems, levels = refs[-4:]
    a, rows = mix.shape[0], stat.shape[0]
    for which, part in enumerate(parts):
        levels[which] = sum(part[pl.ds(a * HD + place * rows, rows), :].astype(jnp.float32) for place in range(3))

    def body(slot):
        every, mixtures = [stat[pl.ds(slot, 1), :]], [mix[slot]]
        for which, (side, part) in enumerate(zip(sides, parts)):
            level = levels[which, pl.ds(slot, 1), :]
            every.append(jnp.where(side_ok(schedule, slot, side), level, jnp.float32(MASKED)))
            mixtures.append(part[pl.ds(pl.multiple_of(slot * HD, HD), HD), :].astype(jnp.float32))
        top = functools.reduce(jnp.maximum, every)
        shares = [jnp.exp2(level - top) for level in every]
        inverse = 1.0 / functools.reduce(jnp.add, shares)
        return functools.reduce(jnp.add, [(share * inverse) * mixture for share, mixture in zip(shares, mixtures)]).T

    store_columns(schedule, 0, a, out, result, sems, body)


def into_columns(kernel, schedule, operands, out, count, scratch, cost, name):
    operands, aliases = (operands, {}) if out is None else ([*operands, out], {1 + len(operands): 0})
    return call(
        kernel,
        schedule,
        operands,
        [jax.ShapeDtypeStruct((ROWS, HEADS * HD), jnp.bfloat16)],
        scratch=[pltpu.VMEM((count, ROWS, HD), jnp.bfloat16), pltpu.SemaphoreType.DMA((count,)), *scratch],
        specs=[VMEM] * (len(operands) - len(aliases)) + [ANY] * len(aliases),
        out_specs=[ANY],
        aliases=aliases,
        cost=cost,
        name=name,
    )[0]


def after(value, *earlier):
    return lax.optimization_barrier((value, *earlier))[0]


def branch(a, b, c, time_tiles, q, k, v, schedule):
    count = time_tiles * HT
    if time_tiles == 2:
        routes = [[(i, (i + HT) % count) for i in range(count)]]
        sides = [None]
    else:
        routes = [[(i, i + HT) for i in range(count - HT)], [(i + HT, i) for i in range(count - HT)]]
        sides = [0, 1]
    backs = [[(there, here) for here, there in route] for route in routes]
    upward = [(i, i + 1) for i in range(count - 1) if i % HT != HT - 1]
    downward = [(there, here) for here, there in upward]

    def move(value, pairs):
        return lax.ppermute(value, "context", pairs)

    d = HEADS - a - b - c
    apart = a >= 2 * b and not d
    (queries,) = pack(schedule, [q], [(0, a)], True, PACK_LIMIT)
    sent = [move(queries, route) for route in routes]
    pieces = pack(schedule, after([k, v], queries), [(0, a), (a, b), (a + b, c)], apart)
    nears = [pieces.pop(0) for _ in range(2 if apart else 1)]
    across = pieces.pop(0) if b else None
    later = pieces.pop(0) if c else None
    near = [move(piece, pairs) for pairs in (upward, downward) for piece in nears]
    early = a > 3
    out, ready = None, schedule
    if d:
        kernel = functools.partial(alone_kernel, a + b + c)
        first = after(schedule, *(nears if early else sent))
        out = into_columns(kernel, first, [q, k, v], None, d, [], hint(FILL_EARLY if early else FILL), "alone")
        ready = schedule if early else after(schedule, out)
    if b:
        across = after(across, *(sent if a == 5 else []), *([out] if d and early else sent))
        others = [move(across, pairs) for pairs in routes]
    parts = [partial_attention(ready, query, k, v, near) for query in sent]
    if c:
        later = after(later, *(sent if a == 5 else []), *([out] if d else sent))
        heights = [move(later, upward), move(later, downward)]
    mix, stat = local_attention(after(schedule, *parts), q, k, v, near, a)
    parts = [move(part, back) for part, back in zip(parts, backs)]
    if b:
        kernel = functools.partial(timed_kernel, a, sides)
        out = into_columns(kernel, after(schedule, stat), [q, k, v, *others], out, b, [], hint(WAIT if a < 6 else 0), "timed")
    if c:
        kernel = functools.partial(tall_kernel, a + b)
        out = into_columns(kernel, after(schedule, stat), [q, k, v, *heights], out, c, [], LONG, "tall")
    scratch = [pltpu.VMEM((len(sides), levels_of(a), ROWS), jnp.float32)]
    return into_columns(
        functools.partial(combine_kernel, sides[::-1]), schedule, [mix, stat, *parts], out, a, scratch, LONG, "combine"
    )


def local(query_rows, key_rows, value_rows, extents):
    time_tiles = lax.axis_size("context") // HT
    index = lax.axis_index("context").astype(jnp.int32).reshape(1)
    schedule, choice = plan(extents, index, time_tiles)
    branches = [functools.partial(branch, *sizes, time_tiles) for sizes in MENU]
    return lax.switch(choice.reshape(()), branches, query_rows, key_rows, value_rows, schedule)


def solution(mesh):
    placed = P(("groups", "context"), None)
    return jax.shard_map(local, mesh=mesh, in_specs=(placed, placed, placed, P()), out_specs=placed, check_vma=False)
```

```python
import functools
import math

import jax
import jax.numpy as jnp
from jax import lax
from jax.experimental import pallas as pl
from jax.experimental.pallas import tpu as pltpu
from jax.sharding import PartitionSpec as P

HEADS = 12
HD = 128
HT = 8
ROWS = 256
MASKED = -1e30
SCALE2 = math.log2(math.e) / math.sqrt(HD)
PACK_LIMIT = 62
FILL_EARLY, FILL, WAIT = 2e10, 1e9, 8e9
MENU = ((2, 2, 3), (3, 2, 3), (3, 2, 4), (4, 2, 3), (4, 2, 4), (5, 2, 4), (6, 2, 3), (7, 2, 2), (9, 1, 1), (12, 0, 0))

TALL, WIDE, TIMED, UP_OK, DOWN_OK, SIDE_OK = 12, 24, 36, 48, 49, 50
SCHEDULE = 64
ANY = pl.BlockSpec(memory_space=pl.ANY)
VMEM = pl.BlockSpec(memory_space=pltpu.VMEM)
SMEM = pl.BlockSpec(memory_space=pltpu.SMEM)


def plan_kernel(time_tiles, extents, index, schedule, chosen):
    one, none = jnp.int32(1), jnp.int32(0)
    wide, timed, tall = [], [], []
    for head in range(HEADS):
        wide.append(jnp.where((extents[2, head] - 1) // 2 >= 0, one, none))
        timed.append(jnp.where((extents[0, head] - 1) // 2 >= 1, one, none))
        tall.append(jnp.where((extents[1, head] - 1) // 2 >= 1, one, none))
    both = sum(t * h for t, h in zip(timed, tall))
    only_timed = sum(timed) - both
    only_tall = sum(tall) - both
    choice, a, b, c = (jnp.int32(x) for x in (len(MENU) - 1, *MENU[-1]))
    for place in reversed(range(len(MENU) - 1)):
        sizes = MENU[place]
        fits = both + jnp.maximum(only_timed - sizes[1], 0) + jnp.maximum(only_tall - sizes[2], 0) <= sizes[0]
        choice, a, b, c = (jnp.where(fits, jnp.int32(x), y) for x, y in zip((place, *sizes), (choice, a, b, c)))
    timed_in_a = jnp.maximum(only_timed - b, 0)
    tall_in_a = jnp.maximum(only_tall - c, 0)
    end_a = both + timed_in_a + tall_in_a
    end_b = a + only_timed - timed_in_a
    end_c = a + b + only_tall - tall_in_a
    seen = [none] * 4
    for head in range(HEADS):
        t, h = timed[head] == 1, tall[head] == 1
        rank = jnp.where(t, jnp.where(h, seen[0], seen[1]), jnp.where(h, seen[2], seen[3]))
        from_timed = jnp.where(rank < timed_in_a, both + rank, a + rank - timed_in_a)
        from_tall = jnp.where(rank < tall_in_a, both + timed_in_a + rank, a + b + rank - tall_in_a)
        left = rank - (a - end_a)
        later = left - (a + b - end_b)
        last = later - (a + b + c - end_c)
        free = jnp.where(
            left < 0, end_a + rank, jnp.where(later < 0, end_b + left, jnp.where(last < 0, end_c + later, a + b + c + last))
        )
        place = jnp.where(t, jnp.where(h, rank, from_timed), jnp.where(h, from_tall, free))
        for kind, is_kind in enumerate((t & h, t & ~h, ~t & h, ~t & ~h)):
            seen[kind] = seen[kind] + jnp.where(is_kind, one, none)
        schedule[place] = jnp.int32(head)
        schedule[TALL + place] = tall[head]
        schedule[WIDE + place] = wide[head]
        schedule[TIMED + place] = timed[head]
    time_index, height_index = lax.div(index[0], jnp.int32(HT)), lax.rem(index[0], jnp.int32(HT))
    schedule[UP_OK] = jnp.where(height_index > 0, one, none)
    schedule[DOWN_OK] = jnp.where(height_index < HT - 1, one, none)
    schedule[SIDE_OK] = jnp.where(time_index > 0, one, none)
    schedule[SIDE_OK + 1] = jnp.where(time_index < time_tiles - 1, one, none)
    chosen[0] = choice
    for place in range(SIDE_OK + 2, SCHEDULE):
        schedule[place] = none


def plan(extents, index, time_tiles):
    return pl.pallas_call(
        functools.partial(plan_kernel, time_tiles),
        out_shape=[jax.ShapeDtypeStruct((SCHEDULE,), jnp.int32), jax.ShapeDtypeStruct((1,), jnp.int32)],
        in_specs=[SMEM, SMEM],
        out_specs=[SMEM, SMEM],
        name="plan",
    )(extents.T, index)


def each(count, body):
    def one(place, carry):
        body(place)
        return carry

    if count > 1:
        lax.fori_loop(0, count, one, 0)
    elif count:
        body(0)


def levels_of(a):
    return -(-a // 8) * 8


def columns(schedule, place):
    return pl.ds(pl.multiple_of(schedule[place] * HD, HD), HD)


def call(kernel, schedule, operands, outs, scratch=(), specs=None, out_specs=None, aliases=None, cost=None, name=None, limit=40):
    return pl.pallas_call(
        kernel,
        out_shape=outs,
        grid_spec=pltpu.PrefetchScalarGridSpec(
            num_scalar_prefetch=1,
            in_specs=specs or [VMEM] * len(operands),
            out_specs=out_specs or [VMEM] * len(outs),
            scratch_shapes=list(scratch),
        ),
        input_output_aliases=aliases or {},
        compiler_params=pltpu.CompilerParams(vmem_limit_bytes=limit * 2**20),
        cost_estimate=cost,
        name=name,
    )(schedule, *operands)


LONG = pl.CostEstimate(flops=10**11, bytes_accessed=10**6, transcendentals=0)
SHORT = pl.CostEstimate(flops=10**6, bytes_accessed=10**5, transcendentals=0)


def hint(flops):
    return pl.CostEstimate(flops=int(flops), bytes_accessed=10**5, transcendentals=0)


def pack_kernel(firsts, sources, apart, schedule, *refs):
    inputs, outs, sems = refs[:sources], list(refs[sources:-1]), refs[-1]
    if apart:
        outs[:sources] = [outs[:sources]]

    def copies(act):
        for first, out in zip(firsts, outs):
            for which, source in enumerate(inputs):
                target = out[which] if isinstance(out, list) else out.at[which]

                def one(place):
                    at = columns(schedule, first + place)
                    act(pltpu.make_async_copy(source.at[:, at], target.at[place], sems.at[first + place, which]))

                each(target.shape[0], one)

    copies(lambda copy: copy.start())
    copies(lambda copy: copy.wait())


def pack(schedule, sources, pieces, apart, limit=40):
    pieces = [(first, size) for first, size in pieces if size]
    shapes = [(len(sources), size, ROWS, HD) for _, size in pieces]
    if apart:
        shapes[:1] = [shapes[0][1:]] * len(sources)
    return list(call(
        functools.partial(pack_kernel, [first for first, _ in pieces], len(sources), apart),
        schedule,
        sources,
        [jax.ShapeDtypeStruct(shape, sources[0].dtype) for shape in shapes],
        scratch=[pltpu.SemaphoreType.DMA((HEADS, len(sources)))],
        specs=[ANY] * len(sources),
        cost=SHORT,
        name="pack",
        limit=limit,
    ))


def attend(query, slabs):
    scores, tops = [], []
    for key, _, ok in slabs:
        score = lax.dot_general(key, query, (((1,), (1,)), ((), ())), preferred_element_type=jnp.float32)
        scores.append(score)
        tops.append(jnp.where(ok, jnp.max(score, axis=0, keepdims=True), jnp.float32(MASKED)))
    top = functools.reduce(jnp.maximum, tops)
    total, mixture = None, None
    for score, (_, value, ok) in zip(scores, slabs):
        weight = jnp.exp2((score - jnp.where(ok, top, jnp.float32(-MASKED))) * SCALE2)
        part = jnp.sum(weight, axis=0, keepdims=True)
        mixed = lax.dot_general(
            value, weight.astype(jnp.bfloat16), (((0,), (0,)), ((), ())), preferred_element_type=jnp.float32
        )
        total = part if total is None else total + part
        mixture = mixed if mixture is None else mixture + mixed
    return mixture * (1.0 / total), top * SCALE2 + jnp.log2(total)


def own_slab(schedule, place, k, v):
    at = columns(schedule, place)
    return k[:, at], v[:, at], schedule[WIDE + place] == 1


def tall_slabs(schedule, place, slot, heights):
    tall = schedule[TALL + place]
    if len(heights) == 2:
        heights = [piece.at[which] for piece in heights for which in range(2)]
    return [
        (heights[0][slot], heights[1][slot], tall * schedule[UP_OK] == 1),
        (heights[2][slot], heights[3][slot], tall * schedule[DOWN_OK] == 1),
    ]


def partial_kernel(schedule, q, k, v, *refs):
    heights, (out, levels) = refs[:-2], refs[-2:]
    a = q.shape[0]
    rows = levels.shape[0]
    levels[...] = jnp.zeros_like(levels)

    def body(place):
        slabs = [own_slab(schedule, place, k, v)] + tall_slabs(schedule, place, place, heights)
        mixture, level = attend(q[place], slabs)
        out[pl.ds(pl.multiple_of(place * HD, HD), HD), :] = mixture.astype(out.dtype)
        levels[pl.ds(place, 1), :] = level

    each(a, body)
    level = levels[...]
    pieces = []
    for _ in range(3):
        piece = level.astype(jnp.bfloat16)
        level = level - piece.astype(jnp.float32)
        pieces.append(piece)
    for place, piece in enumerate(pieces):
        out[pl.ds(a * HD + place * rows, rows), :] = piece


def partial_attention(schedule, q, k, v, heights):
    a = q.shape[0]
    return call(
        partial_kernel,
        schedule,
        [q, k, v, *heights],
        [jax.ShapeDtypeStruct((a * HD + 3 * levels_of(a), ROWS), jnp.bfloat16)],
        scratch=[pltpu.VMEM((levels_of(a), ROWS), jnp.float32)],
        cost=SHORT,
        name="partial_attention",
    )[0]


def local_kernel(schedule, q, k, v, *refs):
    heights, (mix, stat) = refs[:-2], refs[-2:]

    def body(place):
        slabs = [own_slab(schedule, place, k, v)] + tall_slabs(schedule, place, place, heights)
        mixture, level = attend(q[:, columns(schedule, place)], slabs)
        mix[place] = mixture
        stat[pl.ds(place, 1), :] = level

    each(mix.shape[0], body)


def local_attention(schedule, q, k, v, heights, a):
    return call(
        local_kernel,
        schedule,
        [q, k, v, *heights],
        [
            jax.ShapeDtypeStruct((a, HD, ROWS), jnp.float32),
            jax.ShapeDtypeStruct((levels_of(a), ROWS), jnp.float32),
        ],
        cost=SHORT,
        name="local_attention",
    )


def alone_kernel(first, schedule, q, k, v, out, result, sems):
    def body(slot):
        place = first + slot
        return attend(q[:, columns(schedule, place)], [own_slab(schedule, place, k, v)])[0].T

    store_columns(schedule, first, result.shape[0], out, result, sems, body)


def store_columns(schedule, first, count, out, result, sems, body):
    def one(slot):
        result[slot] = body(slot).astype(result.dtype)
        pltpu.make_async_copy(result.at[slot], out.at[:, columns(schedule, first + slot)], sems.at[slot]).start()

    def done(slot):
        pltpu.make_async_copy(result.at[slot], out.at[:, columns(schedule, first + slot)], sems.at[slot]).wait()

    each(count, one)
    each(count, done)


def side_ok(schedule, place, side):
    timed = schedule[TIMED + place]
    return (timed if side is None else timed * schedule[SIDE_OK + side]) == 1


def timed_kernel(a, sides, schedule, q, k, v, *refs):
    parts = refs[: len(sides)]
    out, result, sems = refs[-3:]

    def body(slot):
        place = a + slot
        slabs = [own_slab(schedule, place, k, v)]
        for side, part in zip(sides, parts):
            slabs.append((part[0, slot], part[1, slot], side_ok(schedule, place, side)))
        return attend(q[:, columns(schedule, place)], slabs)[0].T

    store_columns(schedule, a, result.shape[0], out, result, sems, body)


def tall_kernel(first, schedule, q, k, v, up, down, *refs):
    out, result, sems = refs[-3:]

    def body(slot):
        place = first + slot
        slabs = [own_slab(schedule, place, k, v)] + tall_slabs(schedule, place, slot, [up, down])
        return attend(q[:, columns(schedule, place)], slabs)[0].T

    store_columns(schedule, first, result.shape[0], out, result, sems, body)


def combine_kernel(sides, schedule, mix, stat, *refs):
    parts = refs[: len(sides)]
    out, result, sems, levels = refs[-4:]
    a, rows = mix.shape[0], stat.shape[0]
    for which, part in enumerate(parts):
        levels[which] = sum(part[pl.ds(a * HD + place * rows, rows), :].astype(jnp.float32) for place in range(3))

    def body(slot):
        every, mixtures = [stat[pl.ds(slot, 1), :]], [mix[slot]]
        for which, (side, part) in enumerate(zip(sides, parts)):
            level = levels[which, pl.ds(slot, 1), :]
            every.append(jnp.where(side_ok(schedule, slot, side), level, jnp.float32(MASKED)))
            mixtures.append(part[pl.ds(pl.multiple_of(slot * HD, HD), HD), :].astype(jnp.float32))
        top = functools.reduce(jnp.maximum, every)
        shares = [jnp.exp2(level - top) for level in every]
        inverse = 1.0 / functools.reduce(jnp.add, shares)
        return functools.reduce(jnp.add, [(share * inverse) * mixture for share, mixture in zip(shares, mixtures)]).T

    store_columns(schedule, 0, a, out, result, sems, body)


def into_columns(kernel, schedule, operands, out, count, scratch, cost, name):
    operands, aliases = (operands, {}) if out is None else ([*operands, out], {1 + len(operands): 0})
    return call(
        kernel,
        schedule,
        operands,
        [jax.ShapeDtypeStruct((ROWS, HEADS * HD), jnp.bfloat16)],
        scratch=[pltpu.VMEM((count, ROWS, HD), jnp.bfloat16), pltpu.SemaphoreType.DMA((count,)), *scratch],
        specs=[VMEM] * (len(operands) - len(aliases)) + [ANY] * len(aliases),
        out_specs=[ANY],
        aliases=aliases,
        cost=cost,
        name=name,
    )[0]


def after(value, *earlier):
    return lax.optimization_barrier((value, *earlier))[0]


def branch(a, b, c, time_tiles, q, k, v, schedule):
    count = time_tiles * HT
    if time_tiles == 2:
        routes = [[(i, (i + HT) % count) for i in range(count)]]
        sides = [None]
    else:
        routes = [[(i, i + HT) for i in range(count - HT)], [(i + HT, i) for i in range(count - HT)]]
        sides = [0, 1]
    backs = [[(there, here) for here, there in route] for route in routes]
    upward = [(i, i + 1) for i in range(count - 1) if i % HT != HT - 1]
    downward = [(there, here) for here, there in upward]

    def move(value, pairs):
        return lax.ppermute(value, "context", pairs)

    d = HEADS - a - b - c
    apart = a >= 2 * b and not d
    (queries,) = pack(schedule, [q], [(0, a)], True, PACK_LIMIT)
    sent = [move(queries, route) for route in routes]
    pieces = pack(schedule, after([k, v], queries), [(0, a), (a, b), (a + b, c)], apart)
    nears = [pieces.pop(0) for _ in range(2 if apart else 1)]
    across = pieces.pop(0) if b else None
    later = pieces.pop(0) if c else None
    near = [move(piece, pairs) for pairs in (upward, downward) for piece in nears]
    early = a > 3
    out, ready = None, schedule
    if d:
        kernel = functools.partial(alone_kernel, a + b + c)
        first = after(schedule, *(nears if early else sent))
        out = into_columns(kernel, first, [q, k, v], None, d, [], hint(FILL_EARLY if early else FILL), "alone")
        ready = schedule if early else after(schedule, out)
    if b:
        across = after(across, *(sent if a == 5 else []), *([out] if d and early else sent))
        others = [move(across, pairs) for pairs in routes]
    parts = [partial_attention(ready, query, k, v, near) for query in sent]
    if c:
        later = after(later, *(sent if a < 6 and a != 4 else []), *([out] if d and early else sent))
        heights = [move(later, upward), move(later, downward)]
    mix, stat = local_attention(after(schedule, *parts), q, k, v, near, a)
    parts = [move(part, back) for part, back in zip(parts, backs)]
    if b:
        kernel = functools.partial(timed_kernel, a, sides)
        out = into_columns(kernel, after(schedule, stat), [q, k, v, *others], out, b, [], hint(WAIT if a < 6 else 0), "timed")
    if c:
        kernel = functools.partial(tall_kernel, a + b)
        out = into_columns(kernel, after(schedule, stat), [q, k, v, *heights], out, c, [], LONG, "tall")
    scratch = [pltpu.VMEM((len(sides), levels_of(a), ROWS), jnp.float32)]
    return into_columns(
        functools.partial(combine_kernel, sides[::-1]), schedule, [mix, stat, *parts], out, a, scratch, LONG, "combine"
    )


def local(query_rows, key_rows, value_rows, extents):
    time_tiles = lax.axis_size("context") // HT
    index = lax.axis_index("context").astype(jnp.int32).reshape(1)
    schedule, choice = plan(extents, index, time_tiles)
    branches = [functools.partial(branch, *sizes, time_tiles) for sizes in MENU]
    return lax.switch(choice.reshape(()), branches, query_rows, key_rows, value_rows, schedule)


def solution(mesh):
    placed = P(("groups", "context"), None)
    return jax.shard_map(local, mesh=mesh, in_specs=(placed, placed, placed, P()), out_specs=placed, check_vma=False)
```

```python
import functools
import math

import jax
import jax.numpy as jnp
from jax import lax
from jax.experimental import pallas as pl
from jax.experimental.pallas import tpu as pltpu
from jax.sharding import PartitionSpec as P

HEADS = 12
HD = 128
HT = 8
ROWS = 256
MASKED = -1e30
SCALE2 = math.log2(math.e) / math.sqrt(HD)
PACK_LIMIT = 62
FILL_EARLY, FILL, WAIT = 2e10, 1e9, 8e9
MENU = ((2, 2, 3), (3, 2, 3), (3, 2, 4), (4, 2, 3), (4, 2, 4), (5, 2, 4), (6, 2, 3), (7, 2, 2), (9, 1, 1), (12, 0, 0))

TALL, WIDE, TIMED, UP_OK, DOWN_OK, SIDE_OK = 12, 24, 36, 48, 49, 50
SCHEDULE = 64
ANY = pl.BlockSpec(memory_space=pl.ANY)
VMEM = pl.BlockSpec(memory_space=pltpu.VMEM)
SMEM = pl.BlockSpec(memory_space=pltpu.SMEM)


def plan_kernel(time_tiles, extents, index, schedule, chosen):
    one, none = jnp.int32(1), jnp.int32(0)
    wide, timed, tall = [], [], []
    for head in range(HEADS):
        wide.append(jnp.where((extents[2, head] - 1) // 2 >= 0, one, none))
        timed.append(jnp.where((extents[0, head] - 1) // 2 >= 1, one, none))
        tall.append(jnp.where((extents[1, head] - 1) // 2 >= 1, one, none))
    both = sum(t * h for t, h in zip(timed, tall))
    only_timed = sum(timed) - both
    only_tall = sum(tall) - both
    choice, a, b, c = (jnp.int32(x) for x in (len(MENU) - 1, *MENU[-1]))
    for place in reversed(range(len(MENU) - 1)):
        sizes = MENU[place]
        fits = both + jnp.maximum(only_timed - sizes[1], 0) + jnp.maximum(only_tall - sizes[2], 0) <= sizes[0]
        choice, a, b, c = (jnp.where(fits, jnp.int32(x), y) for x, y in zip((place, *sizes), (choice, a, b, c)))
    timed_in_a = jnp.maximum(only_timed - b, 0)
    tall_in_a = jnp.maximum(only_tall - c, 0)
    end_a = both + timed_in_a + tall_in_a
    end_b = a + only_timed - timed_in_a
    end_c = a + b + only_tall - tall_in_a
    seen = [none] * 4
    for head in range(HEADS):
        t, h = timed[head] == 1, tall[head] == 1
        rank = jnp.where(t, jnp.where(h, seen[0], seen[1]), jnp.where(h, seen[2], seen[3]))
        from_timed = jnp.where(rank < timed_in_a, both + rank, a + rank - timed_in_a)
        from_tall = jnp.where(rank < tall_in_a, both + timed_in_a + rank, a + b + rank - tall_in_a)
        left = rank - (a - end_a)
        later = left - (a + b - end_b)
        last = later - (a + b + c - end_c)
        free = jnp.where(
            left < 0, end_a + rank, jnp.where(later < 0, end_b + left, jnp.where(last < 0, end_c + later, a + b + c + last))
        )
        place = jnp.where(t, jnp.where(h, rank, from_timed), jnp.where(h, from_tall, free))
        for kind, is_kind in enumerate((t & h, t & ~h, ~t & h, ~t & ~h)):
            seen[kind] = seen[kind] + jnp.where(is_kind, one, none)
        schedule[place] = jnp.int32(head)
        schedule[TALL + place] = tall[head]
        schedule[WIDE + place] = wide[head]
        schedule[TIMED + place] = timed[head]
    time_index, height_index = lax.div(index[0], jnp.int32(HT)), lax.rem(index[0], jnp.int32(HT))
    schedule[UP_OK] = jnp.where(height_index > 0, one, none)
    schedule[DOWN_OK] = jnp.where(height_index < HT - 1, one, none)
    schedule[SIDE_OK] = jnp.where(time_index > 0, one, none)
    schedule[SIDE_OK + 1] = jnp.where(time_index < time_tiles - 1, one, none)
    chosen[0] = choice
    for place in range(SIDE_OK + 2, SCHEDULE):
        schedule[place] = none


def plan(extents, index, time_tiles):
    return pl.pallas_call(
        functools.partial(plan_kernel, time_tiles),
        out_shape=[jax.ShapeDtypeStruct((SCHEDULE,), jnp.int32), jax.ShapeDtypeStruct((1,), jnp.int32)],
        in_specs=[SMEM, SMEM],
        out_specs=[SMEM, SMEM],
        name="plan",
    )(extents.T, index)


def each(count, body):
    def one(place, carry):
        body(place)
        return carry

    if count > 1:
        lax.fori_loop(0, count, one, 0)
    elif count:
        body(0)


def levels_of(a):
    return -(-a // 8) * 8


def columns(schedule, place):
    return pl.ds(pl.multiple_of(schedule[place] * HD, HD), HD)


def call(kernel, schedule, operands, outs, scratch=(), specs=None, out_specs=None, aliases=None, cost=None, name=None, limit=40):
    return pl.pallas_call(
        kernel,
        out_shape=outs,
        grid_spec=pltpu.PrefetchScalarGridSpec(
            num_scalar_prefetch=1,
            in_specs=specs or [VMEM] * len(operands),
            out_specs=out_specs or [VMEM] * len(outs),
            scratch_shapes=list(scratch),
        ),
        input_output_aliases=aliases or {},
        compiler_params=pltpu.CompilerParams(vmem_limit_bytes=limit * 2**20),
        cost_estimate=cost,
        name=name,
    )(schedule, *operands)


LONG = pl.CostEstimate(flops=10**11, bytes_accessed=10**6, transcendentals=0)
SHORT = pl.CostEstimate(flops=10**6, bytes_accessed=10**5, transcendentals=0)


def hint(flops):
    return pl.CostEstimate(flops=int(flops), bytes_accessed=10**5, transcendentals=0)


def pack_kernel(firsts, sources, apart, schedule, *refs):
    inputs, outs, sems = refs[:sources], list(refs[sources:-1]), refs[-1]
    if apart:
        outs[:sources] = [outs[:sources]]

    def copies(act):
        for first, out in zip(firsts, outs):
            for which, source in enumerate(inputs):
                target = out[which] if isinstance(out, list) else out.at[which]

                def one(place):
                    at = columns(schedule, first + place)
                    act(pltpu.make_async_copy(source.at[:, at], target.at[place], sems.at[first + place, which]))

                each(target.shape[0], one)

    copies(lambda copy: copy.start())
    copies(lambda copy: copy.wait())


def pack(schedule, sources, pieces, apart, limit=40):
    pieces = [(first, size) for first, size in pieces if size]
    shapes = [(len(sources), size, ROWS, HD) for _, size in pieces]
    if apart:
        shapes[:1] = [shapes[0][1:]] * len(sources)
    return list(call(
        functools.partial(pack_kernel, [first for first, _ in pieces], len(sources), apart),
        schedule,
        sources,
        [jax.ShapeDtypeStruct(shape, sources[0].dtype) for shape in shapes],
        scratch=[pltpu.SemaphoreType.DMA((HEADS, len(sources)))],
        specs=[ANY] * len(sources),
        cost=SHORT,
        name="pack",
        limit=limit,
    ))


def attend(query, slabs):
    scores, tops = [], []
    for key, _, ok in slabs:
        score = lax.dot_general(key, query, (((1,), (1,)), ((), ())), preferred_element_type=jnp.float32)
        scores.append(score)
        tops.append(jnp.where(ok, jnp.max(score, axis=0, keepdims=True), jnp.float32(MASKED)))
    top = functools.reduce(jnp.maximum, tops)
    total, mixture = None, None
    for score, (_, value, ok) in zip(scores, slabs):
        weight = jnp.exp2((score - jnp.where(ok, top, jnp.float32(-MASKED))) * SCALE2)
        part = jnp.sum(weight, axis=0, keepdims=True)
        mixed = lax.dot_general(
            value, weight.astype(jnp.bfloat16), (((0,), (0,)), ((), ())), preferred_element_type=jnp.float32
        )
        total = part if total is None else total + part
        mixture = mixed if mixture is None else mixture + mixed
    return mixture * (1.0 / total), top * SCALE2 + jnp.log2(total)


def own_slab(schedule, place, k, v):
    at = columns(schedule, place)
    return k[:, at], v[:, at], schedule[WIDE + place] == 1


def tall_slabs(schedule, place, slot, heights):
    tall = schedule[TALL + place]
    if len(heights) == 2:
        heights = [piece.at[which] for piece in heights for which in range(2)]
    return [
        (heights[0][slot], heights[1][slot], tall * schedule[UP_OK] == 1),
        (heights[2][slot], heights[3][slot], tall * schedule[DOWN_OK] == 1),
    ]


def partial_kernel(schedule, q, k, v, *refs):
    heights, (out, levels) = refs[:-2], refs[-2:]
    a = q.shape[0]
    rows = levels.shape[0]
    levels[...] = jnp.zeros_like(levels)

    def body(place):
        slabs = [own_slab(schedule, place, k, v)] + tall_slabs(schedule, place, place, heights)
        mixture, level = attend(q[place], slabs)
        out[pl.ds(pl.multiple_of(place * HD, HD), HD), :] = mixture.astype(out.dtype)
        levels[pl.ds(place, 1), :] = level

    each(a, body)
    level = levels[...]
    pieces = []
    for _ in range(3):
        piece = level.astype(jnp.bfloat16)
        level = level - piece.astype(jnp.float32)
        pieces.append(piece)
    for place, piece in enumerate(pieces):
        out[pl.ds(a * HD + place * rows, rows), :] = piece


def partial_attention(schedule, q, k, v, heights):
    a = q.shape[0]
    return call(
        partial_kernel,
        schedule,
        [q, k, v, *heights],
        [jax.ShapeDtypeStruct((a * HD + 3 * levels_of(a), ROWS), jnp.bfloat16)],
        scratch=[pltpu.VMEM((levels_of(a), ROWS), jnp.float32)],
        cost=SHORT,
        name="partial_attention",
    )[0]


def local_kernel(schedule, q, k, v, *refs):
    heights, (mix, stat) = refs[:-2], refs[-2:]

    def body(place):
        slabs = [own_slab(schedule, place, k, v)] + tall_slabs(schedule, place, place, heights)
        mixture, level = attend(q[:, columns(schedule, place)], slabs)
        mix[place] = mixture
        stat[pl.ds(place, 1), :] = level

    each(mix.shape[0], body)


def local_attention(schedule, q, k, v, heights, a):
    return call(
        local_kernel,
        schedule,
        [q, k, v, *heights],
        [
            jax.ShapeDtypeStruct((a, HD, ROWS), jnp.float32),
            jax.ShapeDtypeStruct((levels_of(a), ROWS), jnp.float32),
        ],
        cost=SHORT,
        name="local_attention",
    )


def alone_kernel(first, schedule, q, k, v, out, result, sems):
    def body(slot):
        place = first + slot
        return attend(q[:, columns(schedule, place)], [own_slab(schedule, place, k, v)])[0].T

    store_columns(schedule, first, result.shape[0], out, result, sems, body)


def store_columns(schedule, first, count, out, result, sems, body, unrolled=False):
    def one(slot):
        result[slot] = body(slot).astype(result.dtype)
        pltpu.make_async_copy(result.at[slot], out.at[:, columns(schedule, first + slot)], sems.at[slot]).start()

    def done(slot):
        pltpu.make_async_copy(result.at[slot], out.at[:, columns(schedule, first + slot)], sems.at[slot]).wait()

    if unrolled:
        for slot in range(count):
            one(slot)
    else:
        each(count, one)
    each(count, done)


def side_ok(schedule, place, side):
    timed = schedule[TIMED + place]
    return (timed if side is None else timed * schedule[SIDE_OK + side]) == 1


def timed_kernel(a, sides, schedule, q, k, v, *refs):
    parts = refs[: len(sides)]
    out, result, sems = refs[-3:]

    def body(slot):
        place = a + slot
        slabs = [own_slab(schedule, place, k, v)]
        for side, part in zip(sides, parts):
            slabs.append((part[0, slot], part[1, slot], side_ok(schedule, place, side)))
        return attend(q[:, columns(schedule, place)], slabs)[0].T

    store_columns(schedule, a, result.shape[0], out, result, sems, body)


def tall_kernel(first, schedule, q, k, v, up, down, *refs):
    out, result, sems = refs[-3:]

    def body(slot):
        place = first + slot
        slabs = [own_slab(schedule, place, k, v)] + tall_slabs(schedule, place, slot, [up, down])
        return attend(q[:, columns(schedule, place)], slabs)[0].T

    store_columns(schedule, first, result.shape[0], out, result, sems, body, result.shape[0] == 3)


def combine_kernel(sides, schedule, mix, stat, *refs):
    parts = refs[: len(sides)]
    out, result, sems, levels = refs[-4:]
    a, rows = mix.shape[0], stat.shape[0]
    for which, part in enumerate(parts):
        levels[which] = sum(part[pl.ds(a * HD + place * rows, rows), :].astype(jnp.float32) for place in range(3))

    def body(slot):
        every, mixtures = [stat[pl.ds(slot, 1), :]], [mix[slot]]
        for which, (side, part) in enumerate(zip(sides, parts)):
            level = levels[which, pl.ds(slot, 1), :]
            every.append(jnp.where(side_ok(schedule, slot, side), level, jnp.float32(MASKED)))
            mixtures.append(part[pl.ds(pl.multiple_of(slot * HD, HD), HD), :].astype(jnp.float32))
        top = functools.reduce(jnp.maximum, every)
        shares = [jnp.exp2(level - top) for level in every]
        inverse = 1.0 / functools.reduce(jnp.add, shares)
        return functools.reduce(jnp.add, [(share * inverse) * mixture for share, mixture in zip(shares, mixtures)]).T

    store_columns(schedule, 0, a, out, result, sems, body)


def into_columns(kernel, schedule, operands, out, count, scratch, cost, name):
    operands, aliases = (operands, {}) if out is None else ([*operands, out], {1 + len(operands): 0})
    return call(
        kernel,
        schedule,
        operands,
        [jax.ShapeDtypeStruct((ROWS, HEADS * HD), jnp.bfloat16)],
        scratch=[pltpu.VMEM((count, ROWS, HD), jnp.bfloat16), pltpu.SemaphoreType.DMA((count,)), *scratch],
        specs=[VMEM] * (len(operands) - len(aliases)) + [ANY] * len(aliases),
        out_specs=[ANY],
        aliases=aliases,
        cost=cost,
        name=name,
    )[0]


def after(value, *earlier):
    return lax.optimization_barrier((value, *earlier))[0]


def branch(a, b, c, time_tiles, q, k, v, schedule):
    count = time_tiles * HT
    if time_tiles == 2:
        routes = [[(i, (i + HT) % count) for i in range(count)]]
        sides = [None]
    else:
        routes = [[(i, i + HT) for i in range(count - HT)], [(i + HT, i) for i in range(count - HT)]]
        sides = [0, 1]
    backs = [[(there, here) for here, there in route] for route in routes]
    upward = [(i, i + 1) for i in range(count - 1) if i % HT != HT - 1]
    downward = [(there, here) for here, there in upward]

    def move(value, pairs):
        return lax.ppermute(value, "context", pairs)

    d = HEADS - a - b - c
    apart = a >= 2 * b and not d
    (queries,) = pack(schedule, [q], [(0, a)], True, PACK_LIMIT)
    sent = [move(queries, route) for route in routes]
    pieces = pack(schedule, after([k, v], queries), [(0, a), (a, b), (a + b, c)], apart)
    nears = [pieces.pop(0) for _ in range(2 if apart else 1)]
    across = pieces.pop(0) if b else None
    later = pieces.pop(0) if c else None
    near = [move(piece, pairs) for pairs in (upward, downward) for piece in nears]
    early = a > 3
    out, ready = None, schedule
    if d:
        kernel = functools.partial(alone_kernel, a + b + c)
        first = after(schedule, *(nears if early else sent))
        out = into_columns(kernel, first, [q, k, v], None, d, [], hint(FILL_EARLY if early else FILL), "alone")
        ready = schedule if early else after(schedule, out)
    if b:
        across = after(across, *(sent if a == 5 else []), *([out] if d and early else sent))
        others = [move(across, pairs) for pairs in routes]
    parts = [partial_attention(ready, query, k, v, near) for query in sent]
    if c:
        later = after(later, *(sent if a < 6 and a != 4 else []), *([out] if d and early else sent))
        heights = [move(later, upward), move(later, downward)]
    mix, stat = local_attention(after(schedule, *parts), q, k, v, near, a)
    parts = [move(part, back) for part, back in zip(parts, backs)]
    if b:
        kernel = functools.partial(timed_kernel, a, sides)
        out = into_columns(kernel, after(schedule, stat), [q, k, v, *others], out, b, [], hint(WAIT if a < 6 else 0), "timed")
    if c:
        kernel = functools.partial(tall_kernel, a + b)
        out = into_columns(kernel, after(schedule, stat), [q, k, v, *heights], out, c, [], LONG, "tall")
    scratch = [pltpu.VMEM((len(sides), levels_of(a), ROWS), jnp.float32)]
    return into_columns(
        functools.partial(combine_kernel, sides[::-1]), schedule, [mix, stat, *parts], out, a, scratch, LONG, "combine"
    )


def local(query_rows, key_rows, value_rows, extents):
    time_tiles = lax.axis_size("context") // HT
    index = lax.axis_index("context").astype(jnp.int32).reshape(1)
    schedule, choice = plan(extents, index, time_tiles)
    branches = [functools.partial(branch, *sizes, time_tiles) for sizes in MENU]
    return lax.switch(choice.reshape(()), branches, query_rows, key_rows, value_rows, schedule)


def solution(mesh):
    placed = P(("groups", "context"), None)
    return jax.shard_map(local, mesh=mesh, in_specs=(placed, placed, placed, P()), out_specs=placed, check_vma=False)
```
